256 devices in a mesh: seq: 8 (over y_lo, x), chan: 32 (over y_hi, z, core).
Axes of the slice: x: 4, y: 4 (y_hi: 2, y_lo: 2; y = y_hi * 2 + y_lo), z: 8, core: 2. Of those that a mesh axis runs over, the one named last changes fastest.
Arguments:
- query_in: bfloat16 [2048, 4096], P('seq', 'chan'), may hold values from -6 to 6
- key_in: bfloat16 [2048, 4096], P('seq', 'chan'), may hold values from -6 to 6
- value_in: bfloat16 [2048, 4096], P('seq', 'chan'), may hold values from -6 to 6
- filter_taps: bfloat16 [256, 2048], P('chan', 'seq'), may hold values from -1.05 to 1.05, as said below
- skip_gain: float32 [4096], P('chan'), may hold values from 0.5 to 1.5
- out_weight: bfloat16 [4096, 4096], P('chan'), may hold values from -0.09375 to 0.09375
Outputs:
- mixed_out: bfloat16 [2048, 4096], P('seq', 'chan')
The draws below stay inside these ranges and needn't reach their ends.
Inputs may be any that keep to these rules, and one draw needn't show every extreme that they name: `filter_taps`: taps of every filter; the filters differ in how fast their taps fade with the lag.
All inputs are finite; a program needn't handle non-finite values.
Results may differ from the reference program's by a relative error of at most 0.0057.
Values may be sent and summed in bfloat16 or wider, within the bound.
A program may use at most 64 MiB of HBM per device.

```python
import jax
import jax.numpy as jnp

D = 4096
GROUP_CH = 16
FILTER_GROUPS = 256
SEQUENCE_LENGTH = 2048


def draw_filter_taps(key, part):
    random_key_split = jax.random.split(jax.random.fold_in(key, 11), 6)
    token_positions = jnp.arange(SEQUENCE_LENGTH, dtype=jnp.float32)
    slow_share = 0.5
    slow_group = jax.random.uniform(random_key_split[0], (FILTER_GROUPS,)) < slow_share
    slow_rate = jnp.exp(jax.random.uniform(random_key_split[1], (FILTER_GROUPS,), minval=jnp.log(0.1), maxval=jnp.log(1.0))) / SEQUENCE_LENGTH
    fast_rate = jnp.exp(jax.random.uniform(random_key_split[2], (FILTER_GROUPS,), minval=jnp.log(1.0 / 50.0), maxval=jnp.log(1.0 / 30.0)))
    decay_rate = jnp.where(slow_group, slow_rate, fast_rate)
    decay_profile = jnp.exp(-decay_rate[:, None] * token_positions[None, :])
    spike_location = jax.random.randint(random_key_split[3], (FILTER_GROUPS, 2), 1, SEQUENCE_LENGTH).astype(jnp.float32)
    spike_multiplier = jax.random.uniform(random_key_split[4], (FILTER_GROUPS, 2), minval=0.55, maxval=0.8)
    spike_falloff = jnp.prod(jnp.where(token_positions[None, None, :] >= spike_location[:, :, None], spike_multiplier[:, :, None], 1.0), axis=1)
    decay_profile = decay_profile * spike_falloff
    rough_part = jnp.clip(jax.random.normal(random_key_split[5], (FILTER_GROUPS, SEQUENCE_LENGTH)), -4.0, 4.0)
    scale_inv = jnp.sqrt(jnp.sum(decay_profile * decay_profile, axis=1, keepdims=True))
    return (decay_profile * rough_part / scale_inv).astype(jnp.bfloat16)


def steps_of(key, dims, shards, least, high):
    def one(dim, shards_of):
        steps = jax.random.uniform(jax.random.fold_in(jax.random.fold_in(key, 6), dim), (shards_of,), jnp.float32, least / len(shards), high / len(shards))
        return jnp.repeat(jnp.exp(steps), dims[dim] // shards_of).reshape((-1,) + (1,) * (len(dims) - dim - 1))

    factor_of = one(*shards[0])
    for cut in shards[1:]:
        factor_of = factor_of * one(*cut)
    return factor_of


def noise(own_key, dims, spread, limit, cuts=(), kind=jnp.bfloat16):
    array = spread * jax.random.normal(own_key, dims, jnp.float32)
    if cuts:
        array = array * steps_of(own_key, dims, cuts, -0.22, 0.18)
    return jnp.clip(array, -limit, limit).astype(kind)


def setup_inputs(seed: int = 0) -> dict:
    key_of = jax.random.split(jax.random.key(seed), 7)
    query_in = noise(key_of[0], (SEQUENCE_LENGTH, D), 1.0, 6.0, ((0, 8), (1, 32)))
    key_in = noise(key_of[1], (SEQUENCE_LENGTH, D), 1.0, 6.0, ((0, 8), (1, 32)))
    value_in = noise(key_of[2], (SEQUENCE_LENGTH, D), 1.0, 6.0, ((0, 8), (1, 32)))
    filter_taps = draw_filter_taps(jax.random.fold_in(key_of[6], 71), 0)
    skip_gain = jnp.clip(0.5 + 1.0 * jax.random.uniform(key_of[4], (D,), jnp.float32) ** steps_of(key_of[4], (D,), ((0, 32),), -0.2, 0.2), 0.5, 1.5)
    out_weight = noise(key_of[5], (D, D), D ** -0.5, 0.09375, ((0, 32),))
    return dict(query_in=query_in, key_in=key_in, value_in=value_in, filter_taps=filter_taps, skip_gain=skip_gain, out_weight=out_weight)


def reference(query_in, key_in, value_in, filter_taps, skip_gain, out_weight):
    mixed_in = (key_in.astype(jnp.float32) * value_in.astype(jnp.float32)).astype(jnp.bfloat16)
    signal = mixed_in.astype(jnp.float32).T
    length = signal.shape[1]
    per_channel = jnp.repeat(filter_taps.astype(jnp.float32), GROUP_CH, axis=0)
    spectrum = jnp.fft.rfft(signal, n=2 * length, axis=1) * jnp.fft.rfft(per_channel, n=2 * length, axis=1)
    convolved = jnp.fft.irfft(spectrum, n=2 * length, axis=1)[:, :length].T
    gated = (query_in.astype(jnp.float32) * (convolved + skip_gain[None, :] * mixed_in.astype(jnp.float32))).astype(jnp.bfloat16)
    return jnp.dot(gated, out_weight, preferred_element_type=jnp.float32).astype(jnp.bfloat16)
```

```python
import functools

import jax
import jax.numpy as jnp
from jax import lax
from jax.experimental import pallas as pl
from jax.experimental.pallas import tpu as pltpu
from jax.sharding import PartitionSpec as P

MESH = pl.DeviceIdType.MESH
BF = jnp.bfloat16
F32 = jnp.float32
SEQ = 8
RING = 8
ROWS = 256
WIDTH = 128
GROUP = 16
HALF = 128
CHUNKS = 4
PIECE = HALF // CHUNKS


def aligned(value, multiple):
    return pl.multiple_of(value, multiple)


def wait_bytes(ref, sem):
    pltpu.make_async_copy(ref, ref, sem).wait()


def kernel(
    q_hbm, k_hbm, v_hbm, taps_hbm, gain_hbm, w_hbm, out_ref,
    q_in, k_in, v_in, gain, wbuf,
    m_send, q_send, m_recv, q_recv, taps_recv, tmat, conv, g_send, g_recv, g_rows,
    part_a, part_b,
    sa_up, ra_up, sa_dn, ra_dn, sa_y, ra_y,
    sb_y, rb_y, sb_up, rb_up, sb_dn, rb_dn,
    load_sem, w_sem, w_rs, a2a_sem,
    a_up_sem, a_dn_sem, a_y_sem, b_y_sem, b_up_sem, b_dn_sem, send_sem,
):
    s = lax.axis_index("seq")
    k = lax.axis_index("chan")
    core = k % 2
    z = (k // 2) % RING
    yh = k // (2 * RING)
    mate = k + 1 - 2 * core
    up = yh * (2 * RING) + ((z + 1) % RING) * 2 + core
    down = yh * (2 * RING) + ((z + RING - 1) % RING) * 2 + core
    across = (1 - yh) * (2 * RING) + z * 2 + core

    loads = [
        pltpu.make_async_copy(k_hbm, k_in, load_sem.at[0]),
        pltpu.make_async_copy(v_hbm, v_in, load_sem.at[1]),
        pltpu.make_async_copy(q_hbm, q_in, load_sem.at[2]),
        pltpu.make_async_copy(gain_hbm, gain, load_sem.at[3]),
        pltpu.make_async_copy(taps_hbm, taps_recv.at[s], load_sem.at[4]),
    ]
    for load in loads:
        load.start()

    barrier = pltpu.get_barrier_semaphore()
    greeted = [((s + i) % SEQ, c) for i in range(1, SEQ) for c in (k, mate)]
    greeted += [(s, mate), (s, up), (s, down), (s, across)]
    for target in greeted:
        pl.semaphore_signal(barrier, inc=1, device_id=target, device_id_type=MESH)

    def slot_col(r, yr, c):
        block = ((yh + yr) % 2) * (2 * RING) + ((z + r) % RING) * 2 + c
        return aligned(block * WIDTH, WIDTH)

    own_rows = pl.ds(aligned(core * WIDTH, WIDTH), WIDTH)
    for r in range(RING):
        for yr in range(2):
            slot = pl.ds((2 * r + yr) * WIDTH, WIDTH)
            pltpu.make_async_copy(
                w_hbm.at[:, pl.ds(slot_col(r, yr, core), WIDTH)], wbuf.at[own_rows, slot], w_sem
            ).start()

    loads[0].wait()
    loads[1].wait()
    mixed = (k_in[...].astype(F32) * v_in[...].astype(F32)).astype(BF)
    m_send[...] = mixed.astype(F32).T.astype(BF)
    loads[2].wait()
    q_send[...] = q_in[...].astype(F32).T.astype(BF)
    mine = pl.ds(aligned(s * GROUP, GROUP), GROUP)
    m_recv[mine, :] = m_send[mine, :]
    q_recv[mine, :] = q_send[mine, :]
    loads[3].wait()
    loads[4].wait()

    pl.semaphore_wait(barrier, len(greeted))

    peers = [(s + i) % SEQ for i in range(1, SEQ)]

    def remote(src, dst, send, recv, target):
        copy = pltpu.make_async_remote_copy(
            src_ref=src, dst_ref=dst, send_sem=send, recv_sem=recv,
            device_id=target, device_id_type=MESH,
        )
        copy.start()
        return copy

    for p in peers:
        remote(taps_hbm, taps_recv.at[s], send_sem.at[0], a2a_sem.at[0], (p, k))
    for p in peers:
        rows = pl.ds(aligned(p * GROUP, GROUP), GROUP)
        remote(m_send.at[rows, :], m_recv.at[mine, :], send_sem.at[1], a2a_sem.at[1], (p, k))
    for p in peers:
        rows = pl.ds(aligned(p * GROUP, GROUP), GROUP)
        remote(q_send.at[rows, :], q_recv.at[mine, :], send_sem.at[2], a2a_sem.at[2], (p, k))
    for r in range(RING):
        for yr in range(2):
            slot = pl.ds((2 * r + yr) * WIDTH, WIDTH)
            remote(
                w_hbm.at[:, pl.ds(slot_col(r, yr, 1 - core), WIDTH)], wbuf.at[own_rows, slot],
                send_sem.at[3], w_rs, (s, mate),
            )

    wait_bytes(taps_recv.at[pl.ds(0, SEQ - 1)], a2a_sem.at[0])
    all_taps = taps_recv[...].astype(F32)
    group_row = lax.broadcasted_iota(jnp.int32, all_taps.shape, 1)
    taps = jnp.sum(jnp.where(group_row == s, all_taps, 0.0), axis=1)
    row = lax.broadcasted_iota(jnp.int32, (ROWS, ROWS), 0)
    col = lax.broadcasted_iota(jnp.int32, (ROWS, ROWS), 1)
    upper = col >= row
    before = jnp.zeros((ROWS, ROWS), F32)
    for d in range(SEQ):
        spread = jnp.broadcast_to(taps[d : d + 1, :], (ROWS, ROWS))
        rolled = pltpu.roll(spread, 0, 1, stride=1, stride_axis=0)
        tmat[d] = jnp.where(upper, rolled, before).astype(BF)
        before = rolled

    lane = lax.broadcasted_iota(jnp.int32, (WIDTH, WIDTH), 1)
    line = lax.broadcasted_iota(jnp.int32, (WIDTH, WIDTH), 0)
    picked = jnp.where(lane == s * GROUP + line % GROUP, jnp.broadcast_to(gain[...], (WIDTH, WIDTH)), 0.0)
    row_gain = jnp.sum(picked, axis=1, keepdims=True)

    wait_bytes(m_recv.at[pl.ds(0, GROUP * (SEQ - 1)), :], a2a_sem.at[1])
    conv[...] = jnp.dot(m_recv[...], tmat[0], preferred_element_type=F32)
    for d in range(1, SEQ):
        kept = WIDTH - GROUP * d
        conv[GROUP * d :, :] += jnp.dot(m_recv[:kept, :], tmat[d], preferred_element_type=F32)
    wait_bytes(q_recv.at[pl.ds(0, GROUP * (SEQ - 1)), :], a2a_sem.at[2])
    gated = q_recv[...].astype(F32) * (conv[...] + row_gain * m_recv[...].astype(F32))
    g_send[...] = gated.astype(BF)

    land = pl.ds(aligned(core * WIDTH + s * GROUP, GROUP), GROUP)
    for p in peers:
        rows = pl.ds(aligned(p * GROUP, GROUP), GROUP)
        for c in (k, mate):
            remote(g_send.at[rows, :], g_recv.at[land, :], send_sem.at[4], a2a_sem.at[3], (p, c))
    remote(g_send.at[mine, :], g_recv.at[land, :], send_sem.at[4], a2a_sem.at[3], (s, mate))
    g_recv[land, :] = g_send[mine, :]

    wait_bytes(wbuf.at[pl.ds(0, WIDTH), :], w_sem)
    wait_bytes(wbuf.at[pl.ds(0, WIDTH), :], w_rs)
    wait_bytes(g_recv.at[pl.ds(0, 2 * WIDTH - GROUP), :], a2a_sem.at[3])
    g_rows[...] = g_recv[...].astype(F32).T.astype(BF)

    def product(first, r):
        return jnp.dot(
            g_rows[first : first + HALF, :], wbuf[:, 2 * r * WIDTH : 2 * (r + 1) * WIDTH],
            preferred_element_type=F32,
        )

    def piece(c):
        return pl.ds(c * PIECE, PIECE)

    def hop(send, recv, sems, group, step, c, target):
        return remote(
            send.at[step, piece(c), :], recv.at[step, piece(c), :],
            send_sem.at[group], sems.at[step * CHUNKS + c], target,
        )

    def arrive(recv, sems, step, c):
        wait_bytes(recv.at[step, piece(c), :], sems.at[step * CHUNKS + c])
        return recv[step, piece(c), :].astype(F32)

    sa_up[0] = product(0, 4).astype(BF)
    for c in range(CHUNKS):
        hop(sa_up, ra_up, a_up_sem, 5, 0, c, (s, up))
    sa_dn[0] = product(0, 5).astype(BF)
    for c in range(CHUNKS):
        hop(sa_dn, ra_dn, a_dn_sem, 6, 0, c, (s, down))
    order = (4, 3, 5, 2, 6, 1, 7, 0)
    for r in order:
        both = product(HALF, r)
        part_b[r] = both[:, :WIDTH]
        sb_y[r] = both[:, WIDTH:].astype(BF)
        remote(sb_y.at[r], rb_y.at[r], send_sem.at[7], b_y_sem.at[r], (s, across))
    for r in (3, 6, 2, 7, 1, 0):
        part_a[r] = product(0, r)

    def a_step(t):
        for c in range(CHUNKS):
            if t <= 3:
                got = arrive(ra_up, a_up_sem, t - 1, c)
                sa_up[t, piece(c), :] = (part_a[4 - t, piece(c), :] + got).astype(BF)
                hop(sa_up, ra_up, a_up_sem, 5, t, c, (s, up))
            if t <= 2:
                got = arrive(ra_dn, a_dn_sem, t - 1, c)
                sa_dn[t, piece(c), :] = (part_a[5 + t, piece(c), :] + got).astype(BF)
                hop(sa_dn, ra_dn, a_dn_sem, 6, t, c, (s, down))

    def b_own(r):
        wait_bytes(rb_y.at[r], b_y_sem.at[r])
        part_b[r] = part_b[r] + rb_y[r].astype(F32)

    def b_step(t):
        b_own(4 + t)
        if t <= 2:
            b_own(3 - t)
        for c in range(CHUNKS):
            value = part_b[4 + t, piece(c), :]
            if t > 0:
                value = value + arrive(rb_dn, b_dn_sem, t - 1, c)
            sb_dn[t, piece(c), :] = value.astype(BF)
            hop(sb_dn, rb_dn, b_dn_sem, 8, t, c, (s, down))
            if t <= 2:
                value = part_b[3 - t, piece(c), :]
                if t > 0:
                    value = value + arrive(rb_up, b_up_sem, t - 1, c)
                sb_up[t, piece(c), :] = value.astype(BF)
                hop(sb_up, rb_up, b_up_sem, 9, t, c, (s, up))

    a_step(1)
    b_step(0)
    a_step(2)
    b_step(1)
    a_step(3)
    b_step(2)
    for c in range(CHUNKS):
        total = part_a[0, piece(c), :] + arrive(ra_dn, a_dn_sem, 2, c) + arrive(ra_up, a_up_sem, 3, c)
        part_a[0, piece(c), :] = total
        sa_y[piece(c), :] = total[:, WIDTH:].astype(BF)
        remote(sa_y.at[piece(c), :], ra_y.at[piece(c), :], send_sem.at[10], a_y_sem.at[c], (s, across))
    b_step(3)
    b_own(0)
    for c in range(CHUNKS):
        total = part_b[0, piece(c), :] + arrive(rb_up, b_up_sem, 2, c) + arrive(rb_dn, b_dn_sem, 3, c)
        out_ref[pl.ds(HALF + c * PIECE, PIECE), :] = total.astype(BF)
    for c in range(CHUNKS):
        wait_bytes(ra_y.at[piece(c), :], a_y_sem.at[c])
        total = part_a[0, piece(c), :WIDTH] + ra_y[piece(c), :].astype(F32)
        out_ref[piece(c), :] = total.astype(BF)

    wait_bytes(taps_recv.at[pl.ds(0, SEQ - 1)], send_sem.at[0])
    wait_bytes(m_recv.at[pl.ds(0, GROUP * (SEQ - 1)), :], send_sem.at[1])
    wait_bytes(q_recv.at[pl.ds(0, GROUP * (SEQ - 1)), :], send_sem.at[2])
    wait_bytes(wbuf.at[pl.ds(0, WIDTH), :], send_sem.at[3])
    wait_bytes(g_recv.at[pl.ds(0, 2 * WIDTH - GROUP), :], send_sem.at[4])
    wait_bytes(sa_up, send_sem.at[5])
    wait_bytes(sa_dn, send_sem.at[6])
    wait_bytes(sb_y, send_sem.at[7])
    wait_bytes(sb_dn, send_sem.at[8])
    wait_bytes(sb_up, send_sem.at[9])
    wait_bytes(sa_y, send_sem.at[10])


def body(query_in, key_in, value_in, filter_taps, skip_gain, out_weight):
    dma = pltpu.SemaphoreType.DMA
    hbm = pl.BlockSpec(memory_space=pltpu.MemorySpace.HBM)
    return pl.pallas_call(
        kernel,
        out_shape=jax.ShapeDtypeStruct((ROWS, WIDTH), BF),
        in_specs=[hbm] * 6,
        out_specs=pl.BlockSpec(memory_space=pltpu.VMEM),
        scratch_shapes=[
            pltpu.VMEM((ROWS, WIDTH), BF),
            pltpu.VMEM((ROWS, WIDTH), BF),
            pltpu.VMEM((ROWS, WIDTH), BF),
            pltpu.VMEM((1, WIDTH), F32),
            pltpu.VMEM((2 * WIDTH, 2 * RING * WIDTH), BF),
            pltpu.VMEM((WIDTH, ROWS), BF),
            pltpu.VMEM((WIDTH, ROWS), BF),
            pltpu.VMEM((WIDTH, ROWS), BF),
            pltpu.VMEM((WIDTH, ROWS), BF),
            pltpu.VMEM((SEQ, SEQ, ROWS), BF),
            pltpu.VMEM((SEQ, ROWS, ROWS), BF),
            pltpu.VMEM((WIDTH, ROWS), F32),
            pltpu.VMEM((WIDTH, ROWS), BF),
            pltpu.VMEM((2 * WIDTH, ROWS), BF),
            pltpu.VMEM((ROWS, 2 * WIDTH), BF),
            pltpu.VMEM((RING, HALF, 2 * WIDTH), F32),
            pltpu.VMEM((RING, HALF, WIDTH), F32),
            pltpu.VMEM((4, HALF, 2 * WIDTH), BF),
            pltpu.VMEM((4, HALF, 2 * WIDTH), BF),
            pltpu.VMEM((3, HALF, 2 * WIDTH), BF),
            pltpu.VMEM((3, HALF, 2 * WIDTH), BF),
            pltpu.VMEM((HALF, WIDTH), BF),
            pltpu.VMEM((HALF, WIDTH), BF),
            pltpu.VMEM((RING, HALF, WIDTH), BF),
            pltpu.VMEM((RING, HALF, WIDTH), BF),
            pltpu.VMEM((3, HALF, WIDTH), BF),
            pltpu.VMEM((3, HALF, WIDTH), BF),
            pltpu.VMEM((4, HALF, WIDTH), BF),
            pltpu.VMEM((4, HALF, WIDTH), BF),
            dma((5,)),
            dma,
            dma,
            dma((4,)),
            dma((4 * CHUNKS,)),
            dma((3 * CHUNKS,)),
            dma((CHUNKS,)),
            dma((RING,)),
            dma((3 * CHUNKS,)),
            dma((4 * CHUNKS,)),
            dma((11,)),
        ],
        compiler_params=pltpu.CompilerParams(collective_id=0, has_side_effects=True),
    )(query_in, key_in, value_in, filter_taps, skip_gain.reshape(1, WIDTH), out_weight)


def solution(mesh):
    placed = (
        P("seq", "chan"),
        P("seq", "chan"),
        P("seq", "chan"),
        P("chan", "seq"),
        P("chan"),
        P("chan", None),
    )
    return jax.shard_map(
        body, mesh=mesh, in_specs=placed, out_specs=P("seq", "chan"), check_vma=False
    )
```

```python
import functools

import jax
import jax.numpy as jnp
from jax import lax
from jax.experimental import pallas as pl
from jax.experimental.pallas import tpu as pltpu
from jax.sharding import PartitionSpec as P

MESH = pl.DeviceIdType.MESH
BF = jnp.bfloat16
F32 = jnp.float32
SEQ = 8
RING = 8
ROWS = 256
WIDTH = 128
GROUP = 16
HALF = 128
PLACES = (4, 3, 5, 1, 7, 2, 6, 0)
PAIRS = 4
FIRST_PAIRS = 2
R4, UP3, DOWN3, UP1, DOWN1, UP2, DOWN2 = range(7)


def aligned(value, multiple):
    return pl.multiple_of(value, multiple)


def wait_bytes(ref, sem):
    pltpu.make_async_copy(ref, ref, sem).wait()


def kernel(
    q_hbm, k_hbm, v_hbm, taps_hbm, gain_hbm, w_hbm, out_ref,
    q_in, k_in, v_in, gain, wbuf,
    m_send, q_send, m_recv, q_recv, taps_recv, tmat, conv, g_send, g_recv, g_rows,
    part, out_send, out_recv,
    load_sem, w_near, w_far, a2a_sem, g_sem, out_sem, send_sem,
):
    s = lax.axis_index("seq")
    k = lax.axis_index("chan")
    core = k % 2
    z = (k // 2) % RING
    yh = k // (2 * RING)

    def chan(y, level, c):
        return y * (2 * RING) + ((level + RING) % RING) * 2 + c

    mate = chan(yh, z, 1 - core)
    sharing = [chan(y, z, c) for y in (yh, 1 - yh) for c in (core, 1 - core)]
    near = (s + SEQ // 2) % SEQ
    far_rows = [(near, chan(1 - yh, z, c), c) for c in (core, 1 - core)]

    loads = [
        pltpu.make_async_copy(k_hbm, k_in, load_sem.at[0]),
        pltpu.make_async_copy(v_hbm, v_in, load_sem.at[1]),
        pltpu.make_async_copy(q_hbm, q_in, load_sem.at[2]),
        pltpu.make_async_copy(gain_hbm, gain, load_sem.at[3]),
        pltpu.make_async_copy(taps_hbm, taps_recv.at[s], load_sem.at[4]),
    ]
    for load in loads:
        load.start()

    barrier = pltpu.get_barrier_semaphore()
    greeted = [((s + i) % SEQ, c) for i in range(1, SEQ) for c in sharing]
    greeted += [(s, c) for c in sharing[1:]]
    greeted += [(s, chan(yh, z + i, core)) for i in (1, -1, 2, -2)]
    for target in greeted:
        pl.semaphore_signal(barrier, inc=1, device_id=target, device_id_type=MESH)

    def remote(src, dst, send, recv, target):
        pltpu.make_async_remote_copy(
            src_ref=src, dst_ref=dst, send_sem=send, recv_sem=recv,
            device_id=target, device_id_type=MESH,
        ).start()

    w_rows = pl.ds(aligned((yh * 2 + core) * WIDTH, WIDTH), WIDTH)

    def w_block(place, y, c):
        block = chan(y, z + PLACES[place], c)
        return w_hbm.at[:, pl.ds(aligned(block * WIDTH, WIDTH), WIDTH)]

    def w_slot(place):
        return wbuf.at[w_rows, pl.ds(place * WIDTH, WIDTH)]

    for place in range(RING):
        pltpu.make_async_copy(w_block(place, yh, core), w_slot(place), w_near.at[place // 2]).start()

    loads[0].wait()
    loads[1].wait()
    mixed = (k_in[...].astype(F32) * v_in[...].astype(F32)).astype(BF)
    m_send[...] = mixed.astype(F32).T.astype(BF)
    loads[2].wait()
    q_send[...] = q_in[...].astype(F32).T.astype(BF)
    mine = pl.ds(aligned(s * GROUP, GROUP), GROUP)
    m_recv[mine, :] = m_send[mine, :]
    q_recv[mine, :] = q_send[mine, :]
    loads[3].wait()
    loads[4].wait()

    pl.semaphore_wait(barrier, len(greeted))

    peers = [(s + i) % SEQ for i in range(1, SEQ)]
    for p in peers:
        remote(taps_hbm, taps_recv.at[s], send_sem.at[0], a2a_sem.at[0], (p, k))
    for p in peers:
        rows = pl.ds(aligned(p * GROUP, GROUP), GROUP)
        remote(m_send.at[rows, :], m_recv.at[mine, :], send_sem.at[1], a2a_sem.at[1], (p, k))
    for p in peers:
        rows = pl.ds(aligned(p * GROUP, GROUP), GROUP)
        remote(q_send.at[rows, :], q_recv.at[mine, :], send_sem.at[2], a2a_sem.at[2], (p, k))

    def send_far(pair):
        for place in (2 * pair, 2 * pair + 1):
            for seq, target, c in far_rows:
                remote(
                    w_block(place, 1 - yh, c), w_slot(place), send_sem.at[3], w_far.at[pair],
                    (seq, target),
                )

    for place in range(RING):
        remote(
            w_block(place, yh, 1 - core), w_slot(place), send_sem.at[3], w_far.at[place // 2],
            (s, mate),
        )
    for pair in range(FIRST_PAIRS):
        send_far(pair)

    wait_bytes(taps_recv.at[pl.ds(0, SEQ - 1)], a2a_sem.at[0])
    all_taps = taps_recv[...].astype(F32)
    group_row = lax.broadcasted_iota(jnp.int32, all_taps.shape, 1)
    taps = jnp.sum(jnp.where(group_row == s, all_taps, 0.0), axis=1)
    row = lax.broadcasted_iota(jnp.int32, (ROWS, ROWS), 0)
    col = lax.broadcasted_iota(jnp.int32, (ROWS, ROWS), 1)
    upper = col >= row
    before = jnp.zeros((ROWS, ROWS), F32)
    for d in range(SEQ):
        spread = jnp.broadcast_to(taps[d : d + 1, :], (ROWS, ROWS))
        rolled = pltpu.roll(spread, 0, 1, stride=1, stride_axis=0)
        tmat[d] = jnp.where(upper, rolled, before).astype(BF)
        before = rolled

    lane = lax.broadcasted_iota(jnp.int32, (WIDTH, WIDTH), 1)
    line = lax.broadcasted_iota(jnp.int32, (WIDTH, WIDTH), 0)
    picked = jnp.where(lane == s * GROUP + line % GROUP, jnp.broadcast_to(gain[...], (WIDTH, WIDTH)), 0.0)
    row_gain = jnp.sum(picked, axis=1, keepdims=True)

    wait_bytes(m_recv.at[pl.ds(0, GROUP * (SEQ - 1)), :], a2a_sem.at[1])
    conv[...] = jnp.dot(m_recv[...], tmat[0], preferred_element_type=F32)
    for d in range(1, SEQ):
        kept = WIDTH - GROUP * d
        conv[GROUP * d :, :] += jnp.dot(m_recv[:kept, :], tmat[d], preferred_element_type=F32)
    wait_bytes(q_recv.at[pl.ds(0, GROUP * (SEQ - 1)), :], a2a_sem.at[2])
    gated = q_recv[...].astype(F32) * (conv[...] + row_gain * m_recv[...].astype(F32))
    for h in range(2):
        g_send[h] = gated[:, h * HALF : (h + 1) * HALF].astype(BF)

    land = pl.ds(aligned((yh * 2 + core) * WIDTH + s * GROUP, GROUP), GROUP)
    for h in range(2):
        for p in peers:
            rows = pl.ds(aligned(p * GROUP, GROUP), GROUP)
            for c in sharing:
                remote(g_send.at[h, rows, :], g_recv.at[h, land, :], send_sem.at[4], g_sem.at[h], (p, c))
        for c in sharing[1:]:
            remote(g_send.at[h, mine, :], g_recv.at[h, land, :], send_sem.at[4], g_sem.at[h], (s, c))
        g_recv[h, land, :] = g_send[h, mine, :]
    for pair in range(FIRST_PAIRS, PAIRS):
        send_far(pair)

    def wait_w(pair):
        wait_bytes(wbuf.at[pl.ds(0, WIDTH), pl.ds(0, 2 * WIDTH)], w_near.at[pair])
        wait_bytes(wbuf.at[pl.ds(0, 3 * WIDTH), pl.ds(0, 2 * WIDTH)], w_far.at[pair])

    def product(rows, pair):
        return jnp.dot(
            rows, wbuf[:, 2 * pair * WIDTH : 2 * (pair + 1) * WIDTH], preferred_element_type=F32
        )

    def give(kind, h, value, distance):
        out_send[kind, h] = value.astype(BF)
        remote(
            out_send.at[kind, h], out_recv.at[kind, h], send_sem.at[5], out_sem.at[2 * kind + h],
            (s, chan(yh, z + distance, core)),
        )

    def take(kind, h):
        wait_bytes(out_recv.at[kind, h], out_sem.at[2 * kind + h])
        return out_recv[kind, h].astype(F32)

    for h in range(2):
        wait_bytes(g_recv.at[h, pl.ds(0, 4 * WIDTH - GROUP), :], g_sem.at[h])
        g_rows[h] = g_recv[h].astype(F32).T.astype(BF)
        if h == 0:
            wait_w(0)
        both = product(g_rows[h], 0)
        give(R4, h, both[:, :WIDTH], 2 if h == 0 else -2)
        give(UP3, h, both[:, WIDTH:], 1)
        if h == 0:
            wait_w(1)
        both = product(g_rows[h], 1)
        give(DOWN3, h, both[:, :WIDTH], -1)
        give(UP1, h, both[:, WIDTH:], 1)
    wait_w(2)
    for h in range(2):
        both = product(g_rows[h], 2)
        give(DOWN1, h, both[:, :WIDTH], -1)
        part[0, h] = both[:, WIDTH:]
    wait_w(3)
    for h in range(2):
        both = product(g_rows[h], 3)
        part[1, h] = both[:, :WIDTH]
        part[2, h] = both[:, WIDTH:]

    give(DOWN2, 0, part[1, 0] + take(DOWN3, 0), -2)
    give(UP2, 0, part[0, 0] + take(UP3, 0) + take(R4, 0), 2)
    give(UP2, 1, part[0, 1] + take(UP3, 1), 2)
    give(DOWN2, 1, part[1, 1] + take(DOWN3, 1) + take(R4, 1), -2)
    for h in range(2):
        total = part[2, h] + take(UP1, h) + take(DOWN1, h)
        part[2, h] = total
    for h in range(2):
        total = part[2, h] + take(UP2, h) + take(DOWN2, h)
        out_ref[pl.ds(h * HALF, HALF), :] = total.astype(BF)

    wait_bytes(taps_recv.at[pl.ds(0, SEQ - 1)], send_sem.at[0])
    wait_bytes(m_recv.at[pl.ds(0, GROUP * (SEQ - 1)), :], send_sem.at[1])
    wait_bytes(q_recv.at[pl.ds(0, GROUP * (SEQ - 1)), :], send_sem.at[2])
    wait_bytes(wbuf.at[pl.ds(0, 3 * WIDTH), :], send_sem.at[3])
    wait_bytes(g_recv.at[0, pl.ds(0, 4 * WIDTH - GROUP), :], send_sem.at[4])
    wait_bytes(g_recv.at[1, pl.ds(0, 4 * WIDTH - GROUP), :], send_sem.at[4])
    wait_bytes(out_send, send_sem.at[5])


def body(query_in, key_in, value_in, filter_taps, skip_gain, out_weight):
    dma = pltpu.SemaphoreType.DMA
    hbm = pl.BlockSpec(memory_space=pltpu.MemorySpace.HBM)
    return pl.pallas_call(
        kernel,
        out_shape=jax.ShapeDtypeStruct((ROWS, WIDTH), BF),
        in_specs=[hbm] * 6,
        out_specs=pl.BlockSpec(memory_space=pltpu.VMEM),
        scratch_shapes=[
            pltpu.VMEM((ROWS, WIDTH), BF),
            pltpu.VMEM((ROWS, WIDTH), BF),
            pltpu.VMEM((ROWS, WIDTH), BF),
            pltpu.VMEM((1, WIDTH), F32),
            pltpu.VMEM((4 * WIDTH, RING * WIDTH), BF),
            pltpu.VMEM((WIDTH, ROWS), BF),
            pltpu.VMEM((WIDTH, ROWS), BF),
            pltpu.VMEM((WIDTH, ROWS), BF),
            pltpu.VMEM((WIDTH, ROWS), BF),
            pltpu.VMEM((SEQ, SEQ, ROWS), BF),
            pltpu.VMEM((SEQ, ROWS, ROWS), BF),
            pltpu.VMEM((WIDTH, ROWS), F32),
            pltpu.VMEM((2, WIDTH, HALF), BF),
            pltpu.VMEM((2, 4 * WIDTH, HALF), BF),
            pltpu.VMEM((2, HALF, 4 * WIDTH), BF),
            pltpu.VMEM((3, 2, HALF, WIDTH), F32),
            pltpu.VMEM((7, 2, HALF, WIDTH), BF),
            pltpu.VMEM((7, 2, HALF, WIDTH), BF),
            dma((5,)),
            dma((PAIRS,)),
            dma((PAIRS,)),
            dma((3,)),
            dma((2,)),
            dma((14,)),
            dma((6,)),
        ],
        compiler_params=pltpu.CompilerParams(collective_id=0, has_side_effects=True),
    )(query_in, key_in, value_in, filter_taps, skip_gain.reshape(1, WIDTH), out_weight)


def solution(mesh):
    placed = (
        P("seq", "chan"),
        P("seq", "chan"),
        P("seq", "chan"),
        P("chan", "seq"),
        P("chan"),
        P("chan", None),
    )
    return jax.shard_map(
        body, mesh=mesh, in_specs=placed, out_specs=P("seq", "chan"), check_vma=False
    )
```

```python
import functools

import jax
import jax.numpy as jnp
from jax import lax
from jax.experimental import pallas as pl
from jax.experimental.pallas import tpu as pltpu
from jax.sharding import PartitionSpec as P

MESH = pl.DeviceIdType.MESH
BF = jnp.bfloat16
F32 = jnp.float32
SEQ = 8
RING = 8
ROWS = 256
WIDTH = 128
GROUP = 16
HALF = 128
DEEP = ((4, 3), (5,), (7, 1))
SHALLOW = (2, 6, 0)
FIRST = 2
SUB = 1
PIECE = HALF // SUB
DELTAS = ((1, 2), (0, 2), (1, 1), (1, 3), (1, 0), (0, 1), (0, 3))
R4, UP3, DOWN3, UP1, DOWN1, UP2, DOWN2, OVER2, OVER6, OVER0 = range(10)


def aligned(value, multiple):
    return pl.multiple_of(value, multiple)


def wait_bytes(ref, sem):
    pltpu.make_async_copy(ref, ref, sem).wait()


def kernel(
    q_hbm, k_hbm, v_hbm, taps_hbm, gain_hbm, w_hbm, out_ref,
    q_in, k_in, v_in, gain, w_deep, w_flat,
    m_send, q_send, m_recv, q_recv, taps_recv, tmat, conv, g_send, g_recv, g_rows,
    part, out_send, out_recv,
    load_sem, w_near, w_far, a2a_sem, g_sem, out_sem, send_sem,
):
    s = lax.axis_index("seq")
    k = lax.axis_index("chan")
    core = k % 2
    z = (k // 2) % RING
    yh = k // (2 * RING)

    def chan(y, level, c):
        return y * (2 * RING) + ((level + RING) % RING) * 2 + c

    mate = chan(yh, z, 1 - core)
    sharing = [(chan(y, z, c), yr) for yr, y in ((1, 1 - yh), (0, yh)) for c in (1 - core, core)]
    x, ylo = s % 4, s // 4
    near = ((ylo + 1) % 2) * 4 + x
    peers = [((ylo + dy) % 2) * 4 + (x + dx) % 4 for dy, dx in DELTAS]
    far_rows = [(near, chan(1 - yh, z, c), c) for c in (core, 1 - core)]

    loads = [
        pltpu.make_async_copy(k_hbm, k_in, load_sem.at[0]),
        pltpu.make_async_copy(v_hbm, v_in, load_sem.at[1]),
        pltpu.make_async_copy(q_hbm, q_in, load_sem.at[2]),
        pltpu.make_async_copy(gain_hbm, gain, load_sem.at[3]),
        pltpu.make_async_copy(taps_hbm, taps_recv.at[s], load_sem.at[4]),
    ]
    for load in loads:
        load.start()

    barrier = pltpu.get_barrier_semaphore()
    greeted = [(p, c) for p in peers for c, _ in sharing]
    greeted += [(s, c) for c, _ in sharing[:3]]
    greeted += [(s, chan(yh, z + i, core)) for i in (1, -1, 2, -2)]
    for target in greeted:
        pl.semaphore_signal(barrier, inc=1, device_id=target, device_id_type=MESH)

    def remote(src, dst, send, recv, target):
        pltpu.make_async_remote_copy(
            src_ref=src, dst_ref=dst, send_sem=send, recv_sem=recv,
            device_id=target, device_id_type=MESH,
        ).start()


    def w_block(y, distance, c):
        block = chan(y, z + distance, c)
        return w_hbm.at[:, pl.ds(aligned(block * WIDTH, WIDTH), WIDTH)]

    def w_rows(yr):
        return pl.ds(aligned(yr * 2 * WIDTH + core * WIDTH, WIDTH), WIDTH)

    slots = {r: n for n, r in enumerate(r for group in DEEP for r in group)}

    def deep_slot(r, yr):
        return w_deep.at[w_rows(yr), pl.ds(slots[r] * WIDTH, WIDTH)]

    def flat_slot(n):
        return w_flat.at[w_rows(0), pl.ds(n * WIDTH, WIDTH)]

    flat_blocks = [(yh, r) for r in SHALLOW[:2]] + [(1 - yh, r) for r in SHALLOW[:2]]
    flat_blocks += [(yh, SHALLOW[2]), (1 - yh, SHALLOW[2])]

    for n, group in enumerate(DEEP):
        for r in group:
            pltpu.make_async_copy(w_block(yh, r, core), deep_slot(r, 0), w_near.at[n]).start()
    for n, (y, r) in enumerate(flat_blocks):
        pltpu.make_async_copy(w_block(y, r, core), flat_slot(n), w_near.at[3]).start()

    loads[0].wait()
    loads[1].wait()
    mixed = (k_in[...].astype(F32) * v_in[...].astype(F32)).astype(BF)
    m_send[...] = mixed.astype(F32).T.astype(BF)
    loads[2].wait()
    q_send[...] = q_in[...].astype(F32).T.astype(BF)
    mine = pl.ds(aligned(s * GROUP, GROUP), GROUP)
    m_recv[mine, :] = m_send[mine, :]
    q_recv[mine, :] = q_send[mine, :]
    loads[3].wait()
    loads[4].wait()

    pl.semaphore_wait(barrier, len(greeted))

    for p in peers:
        remote(taps_hbm, taps_recv.at[s], send_sem.at[0], a2a_sem.at[0], (p, k))
    for p in peers:
        rows = pl.ds(aligned(p * GROUP, GROUP), GROUP)
        remote(m_send.at[rows, :], m_recv.at[mine, :], send_sem.at[1], a2a_sem.at[1], (p, k))
    for p in peers:
        rows = pl.ds(aligned(p * GROUP, GROUP), GROUP)
        remote(q_send.at[rows, :], q_recv.at[mine, :], send_sem.at[2], a2a_sem.at[2], (p, k))

    def send_far(n):
        for r in DEEP[n]:
            for seq, target, c in far_rows:
                remote(w_block(1 - yh, r, c), deep_slot(r, 1), send_sem.at[3], w_far.at[n], (seq, target))

    for n in range(FIRST):
        send_far(n)
    for n, group in enumerate(DEEP):
        for r in group:
            remote(w_block(yh, r, 1 - core), deep_slot(r, 0), send_sem.at[3], w_far.at[n], (s, mate))
    for n, (y, r) in enumerate(flat_blocks):
        remote(w_block(y, r, 1 - core), flat_slot(n), send_sem.at[3], w_far.at[3], (s, mate))

    wait_bytes(taps_recv.at[pl.ds(0, SEQ - 1)], a2a_sem.at[0])
    all_taps = taps_recv[...].astype(F32)
    group_row = lax.broadcasted_iota(jnp.int32, all_taps.shape, 1)
    taps = jnp.sum(jnp.where(group_row == s, all_taps, 0.0), axis=1)
    row = lax.broadcasted_iota(jnp.int32, (ROWS, ROWS), 0)
    col = lax.broadcasted_iota(jnp.int32, (ROWS, ROWS), 1)
    upper = col >= row
    before = jnp.zeros((ROWS, ROWS), F32)
    for d in range(SEQ):
        spread = jnp.broadcast_to(taps[d : d + 1, :], (ROWS, ROWS))
        rolled = pltpu.roll(spread, 0, 1, stride=1, stride_axis=0)
        tmat[d] = jnp.where(upper, rolled, before).astype(BF)
        before = rolled

    lane = lax.broadcasted_iota(jnp.int32, (WIDTH, WIDTH), 1)
    line = lax.broadcasted_iota(jnp.int32, (WIDTH, WIDTH), 0)
    picked = jnp.where(lane == s * GROUP + line % GROUP, jnp.broadcast_to(gain[...], (WIDTH, WIDTH)), 0.0)
    row_gain = jnp.sum(picked, axis=1, keepdims=True)

    wait_bytes(m_recv.at[pl.ds(0, GROUP * (SEQ - 1)), :], a2a_sem.at[1])
    conv[...] = jnp.dot(m_recv[...], tmat[0], preferred_element_type=F32)
    for d in range(1, SEQ):
        kept = WIDTH - GROUP * d
        conv[GROUP * d :, :] += jnp.dot(m_recv[:kept, :], tmat[d], preferred_element_type=F32)
    wait_bytes(q_recv.at[pl.ds(0, GROUP * (SEQ - 1)), :], a2a_sem.at[2])
    gated = q_recv[...].astype(F32) * (conv[...] + row_gain * m_recv[...].astype(F32))
    for h in range(2):
        g_send[h] = gated[:, h * HALF : (h + 1) * HALF].astype(BF)

    def land(yr):
        return pl.ds(aligned(yr * 2 * WIDTH + core * WIDTH + s * GROUP, GROUP), GROUP)

    for h in range(2):
        for p in (*peers[:5], None, *peers[5:]):
            rows = mine if p is None else pl.ds(aligned(p * GROUP, GROUP), GROUP)
            for c, yr in sharing if p is not None else sharing[:3]:
                remote(
                    g_send.at[h, rows, :], g_recv.at[h, land(yr), :], send_sem.at[4], g_sem.at[h],
                    (s if p is None else p, c),
                )
        g_recv[h, land(0), :] = g_send[h, mine, :]
    for n in range(FIRST, len(DEEP)):
        send_far(n)

    def wait_deep(n):
        columns = pl.ds(0, len(DEEP[n]) * WIDTH)
        wait_bytes(w_deep.at[pl.ds(0, WIDTH), columns], w_near.at[n])
        wait_bytes(w_deep.at[pl.ds(0, 3 * WIDTH), columns], w_far.at[n])

    def deep(h, n):
        first = slots[DEEP[n][0]] * WIDTH
        return jnp.dot(
            g_rows[h], w_deep[:, first : first + len(DEEP[n]) * WIDTH], preferred_element_type=F32
        )

    def flat(h, n):
        return jnp.dot(
            g_rows[h, :, : 2 * WIDTH], w_flat[:, n * 2 * WIDTH : (n + 1) * 2 * WIDTH],
            preferred_element_type=F32,
        )

    def give(kind, h, c, value, distance):
        piece = pl.ds(c * PIECE, PIECE)
        out_send[kind, h, piece, :] = value.astype(BF)
        target = chan(1 - yh, z, core) if kind >= OVER2 else chan(yh, z + distance, core)
        remote(
            out_send.at[kind, h, piece, :], out_recv.at[kind, h, piece, :],
            send_sem.at[5], out_sem.at[(2 * kind + h) * SUB + c], (s, target),
        )

    def take(kind, h, c):
        piece = pl.ds(c * PIECE, PIECE)
        wait_bytes(out_recv.at[kind, h, piece, :], out_sem.at[(2 * kind + h) * SUB + c])
        return out_recv[kind, h, piece, :].astype(F32)

    def cut(value, c):
        return value[c * PIECE : (c + 1) * PIECE]

    for h in range(2):
        wait_bytes(g_recv.at[h, pl.ds(0, 4 * WIDTH - GROUP), :], g_sem.at[h])
        g_rows[h] = g_recv[h].astype(F32).T.astype(BF)
        if h == 0:
            wait_deep(0)
        both = deep(h, 0)
        for c in range(SUB):
            give(R4, h, c, cut(both[:, :WIDTH], c), 2 if h == 0 else -2)
            give(UP3, h, c, cut(both[:, WIDTH:], c), 1)
        if h == 0:
            wait_deep(1)
        one = deep(h, 1)
        for c in range(SUB):
            give(DOWN3, h, c, cut(one, c), -1)
        if h == 0:
            wait_bytes(w_flat.at[pl.ds(0, WIDTH), :], w_near.at[3])
            wait_bytes(w_flat.at[pl.ds(0, WIDTH), :], w_far.at[3])
        both = flat(h, 1)
        for c in range(SUB):
            give(OVER6, h, c, cut(both[:, WIDTH:], c), 0)
        for c in range(SUB):
            give(OVER2, h, c, cut(both[:, :WIDTH], c), 0)
    for h in range(2):
        both = flat(h, 0)
        part[0, h] = both[:, :WIDTH]
        part[1, h] = both[:, WIDTH:]
    wait_deep(2)
    for h in range(2):
        both = deep(h, 2)
        for c in range(SUB):
            give(DOWN1, h, c, cut(both[:, :WIDTH], c), -1)
        for c in range(SUB):
            give(UP1, h, c, cut(both[:, WIDTH:], c), 1)
    for h in range(2):
        both = flat(h, 2)
        part[2, h] = both[:, :WIDTH]
        for c in range(SUB):
            give(OVER0, h, c, cut(both[:, WIDTH:], c), 0)

    def second(kind, h):
        for c in range(SUB):
            piece = pl.ds(c * PIECE, PIECE)
            if kind == UP2:
                total = part[0, h, piece, :] + take(UP3, h, c) + take(OVER2, h, c)
            else:
                total = part[1, h, piece, :] + take(DOWN3, h, c) + take(OVER6, h, c)
            if (kind == UP2) == (h == 0):
                total = total + take(R4, h, c)
            give(kind, h, c, total, 2 if kind == UP2 else -2)

    second(DOWN2, 0)
    second(UP2, 0)
    second(UP2, 1)
    second(DOWN2, 1)
    for h in range(2):
        for c in range(SUB):
            piece = pl.ds(c * PIECE, PIECE)
            part[2, h, piece, :] = (
                part[2, h, piece, :] + take(UP1, h, c) + take(DOWN1, h, c) + take(OVER0, h, c)
            )
    for h in range(2):
        for c in range(SUB):
            piece = pl.ds(c * PIECE, PIECE)
            total = part[2, h, piece, :] + take(UP2, h, c) + take(DOWN2, h, c)
            out_ref[pl.ds(h * HALF + c * PIECE, PIECE), :] = total.astype(BF)

    wait_bytes(taps_recv.at[pl.ds(0, SEQ - 1)], send_sem.at[0])
    wait_bytes(m_recv.at[pl.ds(0, GROUP * (SEQ - 1)), :], send_sem.at[1])
    wait_bytes(q_recv.at[pl.ds(0, GROUP * (SEQ - 1)), :], send_sem.at[2])
    wait_bytes(w_deep.at[pl.ds(0, 3 * WIDTH), :], send_sem.at[3])
    wait_bytes(w_flat.at[pl.ds(0, WIDTH), :], send_sem.at[3])
    wait_bytes(g_recv.at[0, pl.ds(0, 4 * WIDTH - GROUP), :], send_sem.at[4])
    wait_bytes(g_recv.at[1, pl.ds(0, 4 * WIDTH - GROUP), :], send_sem.at[4])
    wait_bytes(out_send, send_sem.at[5])


def body(query_in, key_in, value_in, filter_taps, skip_gain, out_weight):
    dma = pltpu.SemaphoreType.DMA
    hbm = pl.BlockSpec(memory_space=pltpu.MemorySpace.HBM)
    skip_gain = skip_gain.reshape(1, WIDTH)
    operands = (query_in, key_in, value_in, filter_taps, skip_gain, out_weight)
    operands = [pltpu.with_memory_space_constraint(x, pltpu.MemorySpace.HBM) for x in operands]
    return pl.pallas_call(
        kernel,
        out_shape=jax.ShapeDtypeStruct((ROWS, WIDTH), BF),
        in_specs=[hbm] * 6,
        out_specs=pl.BlockSpec(memory_space=pltpu.VMEM),
        scratch_shapes=[
            pltpu.VMEM((ROWS, WIDTH), BF),
            pltpu.VMEM((ROWS, WIDTH), BF),
            pltpu.VMEM((ROWS, WIDTH), BF),
            pltpu.VMEM((1, WIDTH), F32),
            pltpu.VMEM((4 * WIDTH, 5 * WIDTH), BF),
            pltpu.VMEM((2 * WIDTH, 6 * WIDTH), BF),
            pltpu.VMEM((WIDTH, ROWS), BF),
            pltpu.VMEM((WIDTH, ROWS), BF),
            pltpu.VMEM((WIDTH, ROWS), BF),
            pltpu.VMEM((WIDTH, ROWS), BF),
            pltpu.VMEM((SEQ, SEQ, ROWS), BF),
            pltpu.VMEM((SEQ, ROWS, ROWS), BF),
            pltpu.VMEM((WIDTH, ROWS), F32),
            pltpu.VMEM((2, WIDTH, HALF), BF),
            pltpu.VMEM((2, 4 * WIDTH, HALF), BF),
            pltpu.VMEM((2, HALF, 4 * WIDTH), BF),
            pltpu.VMEM((3, 2, HALF, WIDTH), F32),
            pltpu.VMEM((10, 2, HALF, WIDTH), BF),
            pltpu.VMEM((10, 2, HALF, WIDTH), BF),
            dma((5,)),
            dma((4,)),
            dma((4,)),
            dma((3,)),
            dma((2,)),
            dma((20 * SUB,)),
            dma((6,)),
        ],
        compiler_params=pltpu.CompilerParams(collective_id=0, has_side_effects=True, vmem_limit_bytes=24 * 1024 * 1024),
    )(*operands)


def solution(mesh):
    placed = (
        P("seq", "chan"),
        P("seq", "chan"),
        P("seq", "chan"),
        P("chan", "seq"),
        P("chan"),
        P("chan", None),
    )
    return jax.shard_map(
        body, mesh=mesh, in_specs=placed, out_specs=P("seq", "chan"), check_vma=False
    )
```

```python
import functools

import jax
import jax.numpy as jnp
from jax import lax
from jax.experimental import pallas as pl
from jax.experimental.pallas import tpu as pltpu
from jax.sharding import PartitionSpec as P

MESH = pl.DeviceIdType.MESH
BF = jnp.bfloat16
F32 = jnp.float32
SEQ = 8
RING = 8
ROWS = 256
WIDTH = 128
GROUP = 16
HALF = 128
DEEP = ((4, 3), (5,), (7, 1))
SHALLOW = (2, 6, 0)
FIRST = 2
SUB = 1
PIECE = HALF // SUB
DELTAS = ((1, 2), (0, 2), (1, 1), (1, 3), (1, 0), (0, 1), (0, 3))
R4, UP3, DOWN3, UP1, DOWN1, UP2, DOWN2, OVER2, OVER6, OVER0 = range(10)


def aligned(value, multiple):
    return pl.multiple_of(value, multiple)


def wait_bytes(ref, sem):
    pltpu.make_async_copy(ref, ref, sem).wait()


def kernel(
    q_hbm, k_hbm, v_hbm, taps_hbm, gain_hbm, w_hbm, out_ref,
    q_in, k_in, v_in, gain, w_deep, w_flat,
    m_send, q_send, m_recv, q_recv, taps_in, taps_send, taps_recv, tmat, conv, g_send, g_recv, g_rows,
    part, out_send, out_recv,
    load_sem, w_near, w_far, a2a_sem, g_sem, relay_sem, out_sem, send_sem,
):
    s = lax.axis_index("seq")
    k = lax.axis_index("chan")
    core = k % 2
    z = (k // 2) % RING
    yh = k // (2 * RING)

    def chan(y, level, c):
        return y * (2 * RING) + ((level + RING) % RING) * 2 + c

    mate = chan(yh, z, 1 - core)
    sharing = [(chan(y, z, c), yr) for yr, y in ((1, 1 - yh), (0, yh)) for c in (1 - core, core)]
    x, ylo = s % 4, s // 4
    near = ((ylo + 1) % 2) * 4 + x
    peers = [((ylo + dy) % 2) * 4 + (x + dx) % 4 for dy, dx in DELTAS]
    far_rows = [(near, chan(1 - yh, z, c), c) for c in (core, 1 - core)]

    loads = [
        pltpu.make_async_copy(k_hbm, k_in, load_sem.at[0]),
        pltpu.make_async_copy(v_hbm, v_in, load_sem.at[1]),
        pltpu.make_async_copy(q_hbm, q_in, load_sem.at[2]),
        pltpu.make_async_copy(gain_hbm, gain, load_sem.at[3]),
        pltpu.make_async_copy(taps_hbm, taps_in, load_sem.at[4]),
    ]
    for load in loads:
        load.start()

    barrier = pltpu.get_barrier_semaphore()
    same_core = [(chan(1 - yh, z, core), 1), (k, 0)]
    greeted = [(p, c) for p in peers for c, _ in same_core]
    greeted += [far_rows[1][:2], (s, same_core[0][0]), (s, mate)]
    greeted += [(s, chan(yh, z + i, core)) for i in (1, -1, 2, -2)]
    for target in greeted:
        pl.semaphore_signal(barrier, inc=1, device_id=target, device_id_type=MESH)

    def remote(src, dst, send, recv, target):
        pltpu.make_async_remote_copy(
            src_ref=src, dst_ref=dst, send_sem=send, recv_sem=recv,
            device_id=target, device_id_type=MESH,
        ).start()


    def w_block(y, distance, c):
        block = chan(y, z + distance, c)
        return w_hbm.at[:, pl.ds(aligned(block * WIDTH, WIDTH), WIDTH)]

    def w_rows(yr):
        return pl.ds(aligned(yr * 2 * WIDTH + core * WIDTH, WIDTH), WIDTH)

    slots = {r: n for n, r in enumerate(r for group in DEEP for r in group)}

    def deep_slot(r, yr):
        return w_deep.at[w_rows(yr), pl.ds(slots[r] * WIDTH, WIDTH)]

    def flat_slot(n):
        return w_flat.at[w_rows(0), pl.ds(n * WIDTH, WIDTH)]

    flat_blocks = [(yh, r) for r in SHALLOW[:2]] + [(1 - yh, r) for r in SHALLOW[:2]]
    flat_blocks += [(yh, SHALLOW[2]), (1 - yh, SHALLOW[2])]

    for n, group in enumerate(DEEP):
        for r in group:
            pltpu.make_async_copy(w_block(yh, r, core), deep_slot(r, 0), w_near.at[n]).start()
    for n, (y, r) in enumerate(flat_blocks):
        pltpu.make_async_copy(w_block(y, r, core), flat_slot(n), w_near.at[3]).start()

    loads[0].wait()
    loads[1].wait()
    mixed = (k_in[...].astype(F32) * v_in[...].astype(F32)).astype(BF)
    m_send[...] = mixed.astype(F32).T.astype(BF)
    loads[2].wait()
    q_send[...] = q_in[...].astype(F32).T.astype(BF)
    mine = pl.ds(aligned(s * GROUP, GROUP), GROUP)
    m_recv[mine, :] = m_send[mine, :]
    q_recv[mine, :] = q_send[mine, :]
    loads[3].wait()
    loads[4].wait()
    for n in range(SEQ):
        taps_send[n] = taps_in[n : n + 1, :].astype(F32)
    taps_recv[s] = taps_send[s]

    pl.semaphore_wait(barrier, len(greeted))

    for p in peers:
        remote(taps_send.at[p], taps_recv.at[s], send_sem.at[0], a2a_sem.at[0], (p, k))
    for p in peers:
        rows = pl.ds(aligned(p * GROUP, GROUP), GROUP)
        remote(m_send.at[rows, :], m_recv.at[mine, :], send_sem.at[1], a2a_sem.at[1], (p, k))
    for p in peers:
        rows = pl.ds(aligned(p * GROUP, GROUP), GROUP)
        remote(q_send.at[rows, :], q_recv.at[mine, :], send_sem.at[2], a2a_sem.at[2], (p, k))

    def send_far(n):
        for r in DEEP[n]:
            for seq, target, c in far_rows:
                remote(w_block(1 - yh, r, c), deep_slot(r, 1), send_sem.at[3], w_far.at[n], (seq, target))

    for n in range(FIRST):
        send_far(n)
    for n, group in enumerate(DEEP):
        for r in group:
            remote(w_block(yh, r, 1 - core), deep_slot(r, 0), send_sem.at[3], w_far.at[n], (s, mate))
    for n, (y, r) in enumerate(flat_blocks):
        remote(w_block(y, r, 1 - core), flat_slot(n), send_sem.at[3], w_far.at[3], (s, mate))

    wait_bytes(taps_recv.at[pl.ds(0, SEQ - 1)], a2a_sem.at[0])
    row = lax.broadcasted_iota(jnp.int32, (ROWS, ROWS), 0)
    col = lax.broadcasted_iota(jnp.int32, (ROWS, ROWS), 1)
    upper = col >= row
    before = jnp.zeros((ROWS, ROWS), F32)
    for d in range(SEQ):
        spread = jnp.broadcast_to(taps_recv[d], (ROWS, ROWS))
        rolled = pltpu.roll(spread, 0, 1, stride=1, stride_axis=0)
        tmat[d] = jnp.where(upper, rolled, before).astype(BF)
        before = rolled

    lane = lax.broadcasted_iota(jnp.int32, (WIDTH, WIDTH), 1)
    line = lax.broadcasted_iota(jnp.int32, (WIDTH, WIDTH), 0)
    picked = jnp.where(lane == s * GROUP + line % GROUP, jnp.broadcast_to(gain[...], (WIDTH, WIDTH)), 0.0)
    row_gain = jnp.sum(picked, axis=1, keepdims=True)

    wait_bytes(m_recv.at[pl.ds(0, GROUP * (SEQ - 1)), :], a2a_sem.at[1])
    conv[...] = jnp.dot(m_recv[...], tmat[0], preferred_element_type=F32)
    for d in range(1, SEQ):
        kept = WIDTH - GROUP * d
        conv[GROUP * d :, :] += jnp.dot(m_recv[:kept, :], tmat[d], preferred_element_type=F32)
    wait_bytes(q_recv.at[pl.ds(0, GROUP * (SEQ - 1)), :], a2a_sem.at[2])
    gated = q_recv[...].astype(F32) * (conv[...] + row_gain * m_recv[...].astype(F32))
    for h in range(2):
        g_send[h] = gated[:, h * HALF : (h + 1) * HALF].astype(BF)

    def land(yr):
        return pl.ds(aligned(yr * 2 * WIDTH + core * WIDTH + s * GROUP, GROUP), GROUP)

    for h in range(2):
        for p in (*peers[:5], None, *peers[5:]):
            rows = mine if p is None else pl.ds(aligned(p * GROUP, GROUP), GROUP)
            for c, yr in same_core if p is not None else same_core[:1]:
                remote(
                    g_send.at[h, rows, :], g_recv.at[h, land(yr), :], send_sem.at[4], g_sem.at[h],
                    (s if p is None else p, c),
                )
        g_recv[h, land(0), :] = g_send[h, mine, :]
    for n in range(FIRST, len(DEEP)):
        send_far(n)

    def wait_deep(n):
        columns = pl.ds(0, len(DEEP[n]) * WIDTH)
        wait_bytes(w_deep.at[pl.ds(0, WIDTH), columns], w_near.at[n])
        wait_bytes(w_deep.at[pl.ds(0, 3 * WIDTH), columns], w_far.at[n])

    def deep(h, n):
        first = slots[DEEP[n][0]] * WIDTH
        return jnp.dot(
            g_rows[h], w_deep[:, first : first + len(DEEP[n]) * WIDTH], preferred_element_type=F32
        )

    def flat(h, n):
        return jnp.dot(
            g_rows[h, :, : 2 * WIDTH], w_flat[:, n * 2 * WIDTH : (n + 1) * 2 * WIDTH],
            preferred_element_type=F32,
        )

    def give(kind, h, c, value, distance):
        piece = pl.ds(c * PIECE, PIECE)
        out_send[kind, h, piece, :] = value.astype(BF)
        target = chan(1 - yh, z, core) if kind >= OVER2 else chan(yh, z + distance, core)
        remote(
            out_send.at[kind, h, piece, :], out_recv.at[kind, h, piece, :],
            send_sem.at[5], out_sem.at[(2 * kind + h) * SUB + c], (s, target),
        )

    def take(kind, h, c):
        piece = pl.ds(c * PIECE, PIECE)
        wait_bytes(out_recv.at[kind, h, piece, :], out_sem.at[(2 * kind + h) * SUB + c])
        return out_recv[kind, h, piece, :].astype(F32)

    def cut(value, c):
        return value[c * PIECE : (c + 1) * PIECE]

    def relay(h):
        wait_bytes(g_recv.at[h, pl.ds(0, 2 * WIDTH - GROUP), :], g_sem.at[h])
        for yr in range(2):
            remote(
                g_recv.at[h, w_rows(yr), :], g_recv.at[h, w_rows(yr), :], send_sem.at[6],
                relay_sem.at[h], (s, mate),
            )

    def turn(h):
        wait_bytes(g_recv.at[h, pl.ds(0, 2 * WIDTH), :], relay_sem.at[h])
        g_rows[h] = g_recv[h].astype(F32).T.astype(BF)

    def first(h):
        both = deep(h, 0)
        for c in range(SUB):
            give(R4, h, c, cut(both[:, :WIDTH], c), 2 if h == 0 else -2)
            give(UP3, h, c, cut(both[:, WIDTH:], c), 1)

    def first_down(h):
        one = deep(h, 1)
        for c in range(SUB):
            give(DOWN3, h, c, cut(one, c), -1)

    def over(h):
        both = flat(h, 1)
        for c in range(SUB):
            give(OVER6, h, c, cut(both[:, WIDTH:], c), 0)
        for c in range(SUB):
            give(OVER2, h, c, cut(both[:, :WIDTH], c), 0)

    relay(0)
    wait_deep(0)
    wait_deep(1)
    turn(0)
    first(0)
    first_down(0)
    relay(1)
    wait_bytes(w_flat.at[pl.ds(0, WIDTH), :], w_near.at[3])
    wait_bytes(w_flat.at[pl.ds(0, WIDTH), :], w_far.at[3])
    over(0)
    turn(1)
    first(1)
    first_down(1)
    over(1)
    for h in range(2):
        both = flat(h, 0)
        part[0, h] = both[:, :WIDTH]
        part[1, h] = both[:, WIDTH:]
    wait_deep(2)
    for h in range(2):
        both = deep(h, 2)
        for c in range(SUB):
            give(DOWN1, h, c, cut(both[:, :WIDTH], c), -1)
        for c in range(SUB):
            give(UP1, h, c, cut(both[:, WIDTH:], c), 1)
    for h in range(2):
        both = flat(h, 2)
        part[2, h] = both[:, :WIDTH]
        for c in range(SUB):
            give(OVER0, h, c, cut(both[:, WIDTH:], c), 0)

    def second(kind, h):
        for c in range(SUB):
            piece = pl.ds(c * PIECE, PIECE)
            if kind == UP2:
                total = part[0, h, piece, :] + take(UP3, h, c) + take(OVER2, h, c)
            else:
                total = part[1, h, piece, :] + take(DOWN3, h, c) + take(OVER6, h, c)
            if (kind == UP2) == (h == 0):
                total = total + take(R4, h, c)
            give(kind, h, c, total, 2 if kind == UP2 else -2)

    second(DOWN2, 0)
    second(UP2, 0)
    second(UP2, 1)
    second(DOWN2, 1)
    for h in range(2):
        for c in range(SUB):
            piece = pl.ds(c * PIECE, PIECE)
            part[2, h, piece, :] = (
                part[2, h, piece, :] + take(UP1, h, c) + take(DOWN1, h, c) + take(OVER0, h, c)
            )
    for h in range(2):
        for c in range(SUB):
            piece = pl.ds(c * PIECE, PIECE)
            total = part[2, h, piece, :] + take(UP2, h, c) + take(DOWN2, h, c)
            out_ref[pl.ds(h * HALF + c * PIECE, PIECE), :] = total.astype(BF)

    wait_bytes(taps_recv.at[pl.ds(0, SEQ - 1)], send_sem.at[0])
    wait_bytes(m_recv.at[pl.ds(0, GROUP * (SEQ - 1)), :], send_sem.at[1])
    wait_bytes(q_recv.at[pl.ds(0, GROUP * (SEQ - 1)), :], send_sem.at[2])
    wait_bytes(w_deep.at[pl.ds(0, 3 * WIDTH), :], send_sem.at[3])
    wait_bytes(w_flat.at[pl.ds(0, WIDTH), :], send_sem.at[3])
    wait_bytes(g_recv.at[0, pl.ds(0, 4 * WIDTH - 2 * GROUP), :], send_sem.at[4])
    wait_bytes(g_recv.at[0], send_sem.at[6])
    wait_bytes(out_send, send_sem.at[5])


def body(query_in, key_in, value_in, filter_taps, skip_gain, out_weight):
    dma = pltpu.SemaphoreType.DMA
    hbm = pl.BlockSpec(memory_space=pltpu.MemorySpace.HBM)
    skip_gain = skip_gain.reshape(1, WIDTH)
    operands = (query_in, key_in, value_in, filter_taps, skip_gain, out_weight)
    operands = [pltpu.with_memory_space_constraint(x, pltpu.MemorySpace.HBM) for x in operands]
    return pl.pallas_call(
        kernel,
        out_shape=jax.ShapeDtypeStruct((ROWS, WIDTH), BF),
        in_specs=[hbm] * 6,
        out_specs=pl.BlockSpec(memory_space=pltpu.VMEM),
        scratch_shapes=[
            pltpu.VMEM((ROWS, WIDTH), BF),
            pltpu.VMEM((ROWS, WIDTH), BF),
            pltpu.VMEM((ROWS, WIDTH), BF),
            pltpu.VMEM((1, WIDTH), F32),
            pltpu.VMEM((4 * WIDTH, 5 * WIDTH), BF),
            pltpu.VMEM((2 * WIDTH, 6 * WIDTH), BF),
            pltpu.VMEM((WIDTH, ROWS), BF),
            pltpu.VMEM((WIDTH, ROWS), BF),
            pltpu.VMEM((WIDTH, ROWS), BF),
            pltpu.VMEM((WIDTH, ROWS), BF),
            pltpu.VMEM((SEQ, ROWS), BF),
            pltpu.VMEM((SEQ, 1, ROWS), F32),
            pltpu.VMEM((SEQ, 1, ROWS), F32),
            pltpu.VMEM((SEQ, ROWS, ROWS), BF),
            pltpu.VMEM((WIDTH, ROWS), F32),
            pltpu.VMEM((2, WIDTH, HALF), BF),
            pltpu.VMEM((2, 4 * WIDTH, HALF), BF),
            pltpu.VMEM((2, HALF, 4 * WIDTH), BF),
            pltpu.VMEM((3, 2, HALF, WIDTH), F32),
            pltpu.VMEM((10, 2, HALF, WIDTH), BF),
            pltpu.VMEM((10, 2, HALF, WIDTH), BF),
            dma((5,)),
            dma((4,)),
            dma((4,)),
            dma((3,)),
            dma((2,)),
            dma((2,)),
            dma((20 * SUB,)),
            dma((7,)),
        ],
        compiler_params=pltpu.CompilerParams(collective_id=0, has_side_effects=True, vmem_limit_bytes=24 * 1024 * 1024),
    )(*operands)


def solution(mesh):
    placed = (
        P("seq", "chan"),
        P("seq", "chan"),
        P("seq", "chan"),
        P("chan", "seq"),
        P("chan"),
        P("chan", None),
    )
    return jax.shard_map(
        body, mesh=mesh, in_specs=placed, out_specs=P("seq", "chan"), check_vma=False
    )
```

```python
import functools

import jax
import jax.numpy as jnp
from jax import lax
from jax.experimental import pallas as pl
from jax.experimental.pallas import tpu as pltpu
from jax.sharding import PartitionSpec as P

MESH = pl.DeviceIdType.MESH
BF = jnp.bfloat16
F32 = jnp.float32
SEQ = 8
RING = 8
ROWS = 256
WIDTH = 128
GROUP = 16
HALF = 128
DEEP = ((4, 3), (5,), (7, 1))
SHALLOW = (2, 6, 0)
FIRST = 2
SUB = 1
RELAYED = 1
PIECE = HALF // SUB
DELTAS = ((1, 2), (0, 2), (1, 1), (1, 3), (1, 0), (0, 1), (0, 3))
R4, UP3, DOWN3, UP1, DOWN1, UP2, DOWN2, OVER2, OVER6, OVER0 = range(10)


def aligned(value, multiple):
    return pl.multiple_of(value, multiple)


def wait_bytes(ref, sem):
    pltpu.make_async_copy(ref, ref, sem).wait()


def kernel(
    q_hbm, k_hbm, v_hbm, taps_hbm, gain_hbm, w_hbm, out_ref,
    q_in, k_in, v_in, gain, w_deep, w_flat,
    m_send, q_send, m_recv, q_recv, taps_in, taps_send, taps_recv, tmat, conv, g_send, g_recv, g_rows,
    part, out_send, out_recv,
    load_sem, w_near, w_far, a2a_sem, g_sem, relay_sem, out_sem, send_sem,
):
    s = lax.axis_index("seq")
    k = lax.axis_index("chan")
    core = k % 2
    z = (k // 2) % RING
    yh = k // (2 * RING)

    def chan(y, level, c):
        return y * (2 * RING) + ((level + RING) % RING) * 2 + c

    mate = chan(yh, z, 1 - core)
    sharing = [(chan(y, z, c), yr) for yr, y in ((1, 1 - yh), (0, yh)) for c in (1 - core, core)]
    x, ylo = s % 4, s // 4
    near = ((ylo + 1) % 2) * 4 + x
    peers = [((ylo + dy) % 2) * 4 + (x + dx) % 4 for dy, dx in DELTAS]
    far_rows = [(near, chan(1 - yh, z, c), c) for c in (core, 1 - core)]

    loads = [
        pltpu.make_async_copy(k_hbm, k_in, load_sem.at[0]),
        pltpu.make_async_copy(v_hbm, v_in, load_sem.at[1]),
        pltpu.make_async_copy(q_hbm, q_in, load_sem.at[2]),
        pltpu.make_async_copy(gain_hbm, gain, load_sem.at[3]),
        pltpu.make_async_copy(taps_hbm, taps_in, load_sem.at[4]),
    ]
    for load in loads:
        load.start()

    barrier = pltpu.get_barrier_semaphore()
    same_core = [(chan(1 - yh, z, core), 1), (k, 0)]
    greeted = [(p, c) for p in peers for c, _ in sharing]
    greeted += [(s, c) for c, _ in sharing[:3]]
    greeted += [(s, chan(yh, z + i, core)) for i in (1, -1, 2, -2)]
    for target in greeted:
        pl.semaphore_signal(barrier, inc=1, device_id=target, device_id_type=MESH)

    def remote(src, dst, send, recv, target):
        pltpu.make_async_remote_copy(
            src_ref=src, dst_ref=dst, send_sem=send, recv_sem=recv,
            device_id=target, device_id_type=MESH,
        ).start()


    def w_block(y, distance, c):
        block = chan(y, z + distance, c)
        return w_hbm.at[:, pl.ds(aligned(block * WIDTH, WIDTH), WIDTH)]

    def w_rows(yr):
        return pl.ds(aligned(yr * 2 * WIDTH + core * WIDTH, WIDTH), WIDTH)

    slots = {r: n for n, r in enumerate(r for group in DEEP for r in group)}

    def deep_slot(r, yr):
        return w_deep.at[w_rows(yr), pl.ds(slots[r] * WIDTH, WIDTH)]

    def flat_slot(n):
        return w_flat.at[w_rows(0), pl.ds(n * WIDTH, WIDTH)]

    flat_blocks = [(yh, r) for r in SHALLOW[:2]] + [(1 - yh, r) for r in SHALLOW[:2]]
    flat_blocks += [(yh, SHALLOW[2]), (1 - yh, SHALLOW[2])]

    for n, group in enumerate(DEEP):
        for r in group:
            pltpu.make_async_copy(w_block(yh, r, core), deep_slot(r, 0), w_near.at[n]).start()
    for n, (y, r) in enumerate(flat_blocks):
        pltpu.make_async_copy(w_block(y, r, core), flat_slot(n), w_near.at[3]).start()

    loads[0].wait()
    loads[1].wait()
    mixed = (k_in[...].astype(F32) * v_in[...].astype(F32)).astype(BF)
    m_send[...] = mixed.astype(F32).T.astype(BF)
    loads[2].wait()
    q_send[...] = q_in[...].astype(F32).T.astype(BF)
    mine = pl.ds(aligned(s * GROUP, GROUP), GROUP)
    m_recv[mine, :] = m_send[mine, :]
    q_recv[mine, :] = q_send[mine, :]
    loads[3].wait()
    loads[4].wait()
    for n in range(SEQ):
        taps_send[n] = taps_in[n : n + 1, :].astype(F32)
    taps_recv[s] = taps_send[s]

    pl.semaphore_wait(barrier, len(greeted))

    for p in peers:
        remote(taps_send.at[p], taps_recv.at[s], send_sem.at[0], a2a_sem.at[0], (p, k))
    for p in peers:
        rows = pl.ds(aligned(p * GROUP, GROUP), GROUP)
        remote(m_send.at[rows, :], m_recv.at[mine, :], send_sem.at[1], a2a_sem.at[1], (p, k))
    for p in peers:
        rows = pl.ds(aligned(p * GROUP, GROUP), GROUP)
        remote(q_send.at[rows, :], q_recv.at[mine, :], send_sem.at[2], a2a_sem.at[2], (p, k))

    def send_far(n):
        for r in DEEP[n]:
            for seq, target, c in far_rows:
                remote(w_block(1 - yh, r, c), deep_slot(r, 1), send_sem.at[3], w_far.at[n], (seq, target))

    for n in range(FIRST):
        send_far(n)
    for n, group in enumerate(DEEP):
        for r in group:
            remote(w_block(yh, r, 1 - core), deep_slot(r, 0), send_sem.at[3], w_far.at[n], (s, mate))
    for n, (y, r) in enumerate(flat_blocks):
        remote(w_block(y, r, 1 - core), flat_slot(n), send_sem.at[3], w_far.at[3], (s, mate))

    wait_bytes(taps_recv.at[pl.ds(0, SEQ - 1)], a2a_sem.at[0])
    row = lax.broadcasted_iota(jnp.int32, (ROWS, ROWS), 0)
    col = lax.broadcasted_iota(jnp.int32, (ROWS, ROWS), 1)
    upper = col >= row
    before = jnp.zeros((ROWS, ROWS), F32)
    for d in range(SEQ):
        spread = jnp.broadcast_to(taps_recv[d], (ROWS, ROWS))
        rolled = pltpu.roll(spread, 0, 1, stride=1, stride_axis=0)
        tmat[d] = jnp.where(upper, rolled, before).astype(BF)
        before = rolled

    lane = lax.broadcasted_iota(jnp.int32, (WIDTH, WIDTH), 1)
    line = lax.broadcasted_iota(jnp.int32, (WIDTH, WIDTH), 0)
    picked = jnp.where(lane == s * GROUP + line % GROUP, jnp.broadcast_to(gain[...], (WIDTH, WIDTH)), 0.0)
    row_gain = jnp.sum(picked, axis=1, keepdims=True)

    wait_bytes(m_recv.at[pl.ds(0, GROUP * (SEQ - 1)), :], a2a_sem.at[1])
    conv[...] = jnp.dot(m_recv[...], tmat[0], preferred_element_type=F32)
    for d in range(1, SEQ):
        kept = WIDTH - GROUP * d
        conv[GROUP * d :, :] += jnp.dot(m_recv[:kept, :], tmat[d], preferred_element_type=F32)
    wait_bytes(q_recv.at[pl.ds(0, GROUP * (SEQ - 1)), :], a2a_sem.at[2])
    gated = q_recv[...].astype(F32) * (conv[...] + row_gain * m_recv[...].astype(F32))
    for h in range(2):
        g_send[h] = gated[:, h * HALF : (h + 1) * HALF].astype(BF)

    def land(yr):
        return pl.ds(aligned(yr * 2 * WIDTH + core * WIDTH + s * GROUP, GROUP), GROUP)

    for h in range(2):
        targets = same_core if h == RELAYED else sharing
        for p in (*peers[:5], None, *peers[5:]):
            rows = mine if p is None else pl.ds(aligned(p * GROUP, GROUP), GROUP)
            for c, yr in targets if p is not None else targets[:-1]:
                remote(
                    g_send.at[h, rows, :], g_recv.at[h, land(yr), :], send_sem.at[4], g_sem.at[h],
                    (s if p is None else p, c),
                )
        g_recv[h, land(0), :] = g_send[h, mine, :]
    for n in range(FIRST, len(DEEP)):
        send_far(n)

    def wait_deep(n):
        columns = pl.ds(0, len(DEEP[n]) * WIDTH)
        wait_bytes(w_deep.at[pl.ds(0, WIDTH), columns], w_near.at[n])
        wait_bytes(w_deep.at[pl.ds(0, 3 * WIDTH), columns], w_far.at[n])

    def deep(h, n):
        first = slots[DEEP[n][0]] * WIDTH
        return jnp.dot(
            g_rows[h], w_deep[:, first : first + len(DEEP[n]) * WIDTH], preferred_element_type=F32
        )

    def flat(h, n):
        return jnp.dot(
            g_rows[h, :, : 2 * WIDTH], w_flat[:, n * 2 * WIDTH : (n + 1) * 2 * WIDTH],
            preferred_element_type=F32,
        )

    def give(kind, h, c, value, distance):
        piece = pl.ds(c * PIECE, PIECE)
        out_send[kind, h, piece, :] = value.astype(BF)
        target = chan(1 - yh, z, core) if kind >= OVER2 else chan(yh, z + distance, core)
        remote(
            out_send.at[kind, h, piece, :], out_recv.at[kind, h, piece, :],
            send_sem.at[5], out_sem.at[(2 * kind + h) * SUB + c], (s, target),
        )

    def take(kind, h, c):
        piece = pl.ds(c * PIECE, PIECE)
        wait_bytes(out_recv.at[kind, h, piece, :], out_sem.at[(2 * kind + h) * SUB + c])
        return out_recv[kind, h, piece, :].astype(F32)

    def cut(value, c):
        return value[c * PIECE : (c + 1) * PIECE]

    def relay(h):
        if h != RELAYED:
            return
        wait_bytes(g_recv.at[h, pl.ds(0, 2 * WIDTH - GROUP), :], g_sem.at[h])
        for yr in range(2):
            remote(
                g_recv.at[h, w_rows(yr), :], g_recv.at[h, w_rows(yr), :], send_sem.at[6],
                relay_sem, (s, mate),
            )

    def turn(h):
        if h == RELAYED:
            wait_bytes(g_recv.at[h, pl.ds(0, 2 * WIDTH), :], relay_sem)
        else:
            wait_bytes(g_recv.at[h, pl.ds(0, 4 * WIDTH - GROUP), :], g_sem.at[h])
        g_rows[h] = g_recv[h].astype(F32).T.astype(BF)

    def first(h):
        both = deep(h, 0)
        for c in range(SUB):
            give(R4, h, c, cut(both[:, :WIDTH], c), 2 if h == 0 else -2)
            give(UP3, h, c, cut(both[:, WIDTH:], c), 1)

    def first_down(h):
        one = deep(h, 1)
        for c in range(SUB):
            give(DOWN3, h, c, cut(one, c), -1)

    def over(h):
        both = flat(h, 1)
        for c in range(SUB):
            give(OVER6, h, c, cut(both[:, WIDTH:], c), 0)
        for c in range(SUB):
            give(OVER2, h, c, cut(both[:, :WIDTH], c), 0)

    relay(0)
    wait_deep(0)
    wait_deep(1)
    turn(0)
    first(0)
    first_down(0)
    relay(1)
    wait_bytes(w_flat.at[pl.ds(0, WIDTH), :], w_near.at[3])
    wait_bytes(w_flat.at[pl.ds(0, WIDTH), :], w_far.at[3])
    over(0)
    turn(1)
    first(1)
    first_down(1)
    over(1)
    for h in range(2):
        both = flat(h, 0)
        part[0, h] = both[:, :WIDTH]
        part[1, h] = both[:, WIDTH:]
    wait_deep(2)
    for h in range(2):
        both = deep(h, 2)
        for c in range(SUB):
            give(DOWN1, h, c, cut(both[:, :WIDTH], c), -1)
        for c in range(SUB):
            give(UP1, h, c, cut(both[:, WIDTH:], c), 1)
    for h in range(2):
        both = flat(h, 2)
        part[2, h] = both[:, :WIDTH]
        for c in range(SUB):
            give(OVER0, h, c, cut(both[:, WIDTH:], c), 0)

    def second(kind, h):
        for c in range(SUB):
            piece = pl.ds(c * PIECE, PIECE)
            if kind == UP2:
                total = part[0, h, piece, :] + take(UP3, h, c) + take(OVER2, h, c)
            else:
                total = part[1, h, piece, :] + take(DOWN3, h, c) + take(OVER6, h, c)
            if (kind == UP2) == (h == 0):
                total = total + take(R4, h, c)
            give(kind, h, c, total, 2 if kind == UP2 else -2)

    second(DOWN2, 0)
    second(UP2, 0)
    second(UP2, 1)
    second(DOWN2, 1)
    for h in range(2):
        for c in range(SUB):
            piece = pl.ds(c * PIECE, PIECE)
            part[2, h, piece, :] = (
                part[2, h, piece, :] + take(UP1, h, c) + take(DOWN1, h, c) + take(OVER0, h, c)
            )
    for h in range(2):
        for c in range(SUB):
            piece = pl.ds(c * PIECE, PIECE)
            total = part[2, h, piece, :] + take(UP2, h, c) + take(DOWN2, h, c)
            out_ref[pl.ds(h * HALF + c * PIECE, PIECE), :] = total.astype(BF)

    wait_bytes(taps_recv.at[pl.ds(0, SEQ - 1)], send_sem.at[0])
    wait_bytes(m_recv.at[pl.ds(0, GROUP * (SEQ - 1)), :], send_sem.at[1])
    wait_bytes(q_recv.at[pl.ds(0, GROUP * (SEQ - 1)), :], send_sem.at[2])
    wait_bytes(w_deep.at[pl.ds(0, 3 * WIDTH), :], send_sem.at[3])
    wait_bytes(w_flat.at[pl.ds(0, WIDTH), :], send_sem.at[3])
    wait_bytes(g_recv.at[0, pl.ds(0, 2 * WIDTH - GROUP), :], send_sem.at[4])
    wait_bytes(g_recv.at[0, pl.ds(0, 4 * WIDTH - GROUP), :], send_sem.at[4])
    wait_bytes(g_recv.at[0, pl.ds(0, 2 * WIDTH), :], send_sem.at[6])
    wait_bytes(out_send, send_sem.at[5])


def body(query_in, key_in, value_in, filter_taps, skip_gain, out_weight):
    dma = pltpu.SemaphoreType.DMA
    hbm = pl.BlockSpec(memory_space=pltpu.MemorySpace.HBM)
    skip_gain = skip_gain.reshape(1, WIDTH)
    operands = (query_in, key_in, value_in, filter_taps, skip_gain, out_weight)
    operands = [pltpu.with_memory_space_constraint(x, pltpu.MemorySpace.HBM) for x in operands]
    return pl.pallas_call(
        kernel,
        out_shape=jax.ShapeDtypeStruct((ROWS, WIDTH), BF),
        in_specs=[hbm] * 6,
        out_specs=pl.BlockSpec(memory_space=pltpu.VMEM),
        scratch_shapes=[
            pltpu.VMEM((ROWS, WIDTH), BF),
            pltpu.VMEM((ROWS, WIDTH), BF),
            pltpu.VMEM((ROWS, WIDTH), BF),
            pltpu.VMEM((1, WIDTH), F32),
            pltpu.VMEM((4 * WIDTH, 5 * WIDTH), BF),
            pltpu.VMEM((2 * WIDTH, 6 * WIDTH), BF),
            pltpu.VMEM((WIDTH, ROWS), BF),
            pltpu.VMEM((WIDTH, ROWS), BF),
            pltpu.VMEM((WIDTH, ROWS), BF),
            pltpu.VMEM((WIDTH, ROWS), BF),
            pltpu.VMEM((SEQ, ROWS), BF),
            pltpu.VMEM((SEQ, 1, ROWS), F32),
            pltpu.VMEM((SEQ, 1, ROWS), F32),
            pltpu.VMEM((SEQ, ROWS, ROWS), BF),
            pltpu.VMEM((WIDTH, ROWS), F32),
            pltpu.VMEM((2, WIDTH, HALF), BF),
            pltpu.VMEM((2, 4 * WIDTH, HALF), BF),
            pltpu.VMEM((2, HALF, 4 * WIDTH), BF),
            pltpu.VMEM((3, 2, HALF, WIDTH), F32),
            pltpu.VMEM((10, 2, HALF, WIDTH), BF),
            pltpu.VMEM((10, 2, HALF, WIDTH), BF),
            dma((5,)),
            dma((4,)),
            dma((4,)),
            dma((3,)),
            dma((2,)),
            dma,
            dma((20 * SUB,)),
            dma((7,)),
        ],
        compiler_params=pltpu.CompilerParams(collective_id=0, has_side_effects=True, vmem_limit_bytes=24 * 1024 * 1024),
    )(*operands)


def solution(mesh):
    placed = (
        P("seq", "chan"),
        P("seq", "chan"),
        P("seq", "chan"),
        P("chan", "seq"),
        P("chan"),
        P("chan", None),
    )
    return jax.shard_map(
        body, mesh=mesh, in_specs=placed, out_specs=P("seq", "chan"), check_vma=False
    )
```

```python
import functools

import jax
import jax.numpy as jnp
from jax import lax
from jax.experimental import pallas as pl
from jax.experimental.pallas import tpu as pltpu
from jax.sharding import PartitionSpec as P

MESH = pl.DeviceIdType.MESH
BF = jnp.bfloat16
F32 = jnp.float32
SEQ = 8
RING = 8
ROWS = 256
WIDTH = 128
GROUP = 16
HALF = 128
DEEP = ((4, 3), (5,), (7, 1))
SHALLOW = (2, 6, 0)
FIRST = 2
SUB = 1
RELAYED = 1
PIECE = HALF // SUB
DELTAS = ((1, 2), (0, 2), (1, 1), (1, 3), (1, 0), (0, 1), (0, 3))
R4, UP3, DOWN3, UP1, DOWN1, UP2, DOWN2, OVER2, OVER6, OVER0 = range(10)


def aligned(value, multiple):
    return pl.multiple_of(value, multiple)


def wait_bytes(ref, sem):
    pltpu.make_async_copy(ref, ref, sem).wait()


def kernel(
    q_hbm, k_hbm, v_hbm, taps_hbm, gain_hbm, w_hbm, out_ref,
    q_in, k_in, v_in, gain, w_deep, w_flat,
    m_send, q_send, m_recv, q_recv, taps_in, taps_send, taps_recv, tmat, conv, g_send, g_recv, g_rows,
    part, out_send, out_recv,
    load_sem, w_near, w_far, a2a_sem, g_sem, relay_sem, out_sem, send_sem,
):
    s = lax.axis_index("seq")
    k = lax.axis_index("chan")
    core = k % 2
    z = (k // 2) % RING
    yh = k // (2 * RING)

    def chan(y, level, c):
        return y * (2 * RING) + ((level + RING) % RING) * 2 + c

    mate = chan(yh, z, 1 - core)
    sharing = [(chan(y, z, c), yr) for yr, y in ((1, 1 - yh), (0, yh)) for c in (1 - core, core)]
    x, ylo = s % 4, s // 4
    near = ((ylo + 1) % 2) * 4 + x
    peers = [((ylo + dy) % 2) * 4 + (x + dx) % 4 for dy, dx in DELTAS]
    far_rows = [(near, chan(1 - yh, z, c), c) for c in (core, 1 - core)]

    loads = [
        pltpu.make_async_copy(k_hbm, k_in, load_sem.at[0]),
        pltpu.make_async_copy(v_hbm, v_in, load_sem.at[1]),
        pltpu.make_async_copy(q_hbm, q_in, load_sem.at[2]),
        pltpu.make_async_copy(gain_hbm, gain, load_sem.at[3]),
        pltpu.make_async_copy(taps_hbm, taps_in, load_sem.at[4]),
    ]
    for load in loads:
        load.start()

    barrier = pltpu.get_barrier_semaphore()
    same_core = [(chan(1 - yh, z, core), 1), (k, 0)]
    greeted = [(p, c) for p in peers for c, _ in sharing]
    greeted += [(s, c) for c, _ in sharing[:3]]
    greeted += [(s, chan(yh, z + i, core)) for i in (1, -1, 2, -2)]
    for target in greeted:
        pl.semaphore_signal(barrier, inc=1, device_id=target, device_id_type=MESH)

    def remote(src, dst, send, recv, target):
        pltpu.make_async_remote_copy(
            src_ref=src, dst_ref=dst, send_sem=send, recv_sem=recv,
            device_id=target, device_id_type=MESH,
        ).start()


    def w_block(y, distance, c):
        block = chan(y, z + distance, c)
        return w_hbm.at[:, pl.ds(aligned(block * WIDTH, WIDTH), WIDTH)]

    def w_rows(yr):
        return pl.ds(aligned(yr * 2 * WIDTH + core * WIDTH, WIDTH), WIDTH)

    slots = {r: n for n, r in enumerate(r for group in DEEP for r in group)}

    def deep_slot(r, yr):
        return w_deep.at[w_rows(yr), pl.ds(slots[r] * WIDTH, WIDTH)]

    def flat_slot(n):
        return w_flat.at[w_rows(0), pl.ds(n * WIDTH, WIDTH)]

    flat_blocks = [(yh, r) for r in SHALLOW[:2]] + [(1 - yh, r) for r in SHALLOW[:2]]
    flat_blocks += [(yh, SHALLOW[2]), (1 - yh, SHALLOW[2])]

    loads[0].wait()
    loads[1].wait()
    mixed = (k_in[...].astype(F32) * v_in[...].astype(F32)).astype(BF)
    m_send[...] = mixed.astype(F32).T.astype(BF)
    mine = pl.ds(aligned(s * GROUP, GROUP), GROUP)
    loads[3].wait()
    loads[4].wait()
    for n in range(SEQ):
        taps_send[n] = taps_in[n : n + 1, :].astype(F32)
    taps_recv[s] = taps_send[s]

    pl.semaphore_wait(barrier, len(greeted))

    for p in peers:
        remote(taps_send.at[p], taps_recv.at[s], send_sem.at[0], a2a_sem.at[0], (p, k))
    for p in peers:
        rows = pl.ds(aligned(p * GROUP, GROUP), GROUP)
        remote(m_send.at[rows, :], m_recv.at[mine, :], send_sem.at[1], a2a_sem.at[1], (p, k))
    loads[2].wait()
    q_send[...] = q_in[...].astype(F32).T.astype(BF)
    for p in peers:
        rows = pl.ds(aligned(p * GROUP, GROUP), GROUP)
        remote(q_send.at[rows, :], q_recv.at[mine, :], send_sem.at[2], a2a_sem.at[2], (p, k))

    def send_far(n):
        for r in DEEP[n]:
            for seq, target, c in far_rows:
                remote(w_block(1 - yh, r, c), deep_slot(r, 1), send_sem.at[3], w_far.at[n], (seq, target))

    for n in range(FIRST):
        send_far(n)
    for n, group in enumerate(DEEP):
        for r in group:
            remote(w_block(yh, r, 1 - core), deep_slot(r, 0), send_sem.at[3], w_far.at[n], (s, mate))
    for n, (y, r) in enumerate(flat_blocks):
        remote(w_block(y, r, 1 - core), flat_slot(n), send_sem.at[3], w_far.at[3], (s, mate))

    m_recv[mine, :] = m_send[mine, :]
    q_recv[mine, :] = q_send[mine, :]
    for n, group in enumerate(DEEP):
        for r in group:
            pltpu.make_async_copy(w_block(yh, r, core), deep_slot(r, 0), w_near.at[n]).start()
    for n, (y, r) in enumerate(flat_blocks):
        pltpu.make_async_copy(w_block(y, r, core), flat_slot(n), w_near.at[3]).start()

    wait_bytes(taps_recv.at[pl.ds(0, SEQ - 1)], a2a_sem.at[0])
    row = lax.broadcasted_iota(jnp.int32, (ROWS, ROWS), 0)
    col = lax.broadcasted_iota(jnp.int32, (ROWS, ROWS), 1)
    upper = col >= row
    before = jnp.zeros((ROWS, ROWS), F32)
    for d in range(SEQ):
        spread = jnp.broadcast_to(taps_recv[d], (ROWS, ROWS))
        rolled = pltpu.roll(spread, 0, 1, stride=1, stride_axis=0)
        tmat[d] = jnp.where(upper, rolled, before).astype(BF)
        before = rolled

    lane = lax.broadcasted_iota(jnp.int32, (WIDTH, WIDTH), 1)
    line = lax.broadcasted_iota(jnp.int32, (WIDTH, WIDTH), 0)
    picked = jnp.where(lane == s * GROUP + line % GROUP, jnp.broadcast_to(gain[...], (WIDTH, WIDTH)), 0.0)
    row_gain = jnp.sum(picked, axis=1, keepdims=True)

    wait_bytes(m_recv.at[pl.ds(0, GROUP * (SEQ - 1)), :], a2a_sem.at[1])
    skip = row_gain * m_recv[...].astype(F32)

    def gate(h):
        side = slice(h * HALF, (h + 1) * HALF)
        conv[:, side] = jnp.dot(m_recv[...], tmat[0, :, side], preferred_element_type=F32)
        for d in range(1, SEQ):
            kept = WIDTH - GROUP * d
            conv[GROUP * d :, side] += jnp.dot(
                m_recv[:kept, :], tmat[d, :, side], preferred_element_type=F32
            )
        if h == 0:
            wait_bytes(q_recv.at[pl.ds(0, GROUP * (SEQ - 1)), :], a2a_sem.at[2])
        g_send[h] = (q_recv[:, side].astype(F32) * (conv[:, side] + skip[:, side])).astype(BF)

    def land(yr):
        return pl.ds(aligned(yr * 2 * WIDTH + core * WIDTH + s * GROUP, GROUP), GROUP)

    for h in range(2):
        gate(h)
        targets = same_core if h == RELAYED else sharing
        for p in (*peers[:5], None, *peers[5:]):
            rows = mine if p is None else pl.ds(aligned(p * GROUP, GROUP), GROUP)
            for c, yr in targets if p is not None else targets[:-1]:
                remote(
                    g_send.at[h, rows, :], g_recv.at[h, land(yr), :], send_sem.at[4], g_sem.at[h],
                    (s if p is None else p, c),
                )
        g_recv[h, land(0), :] = g_send[h, mine, :]
    for n in range(FIRST, len(DEEP)):
        send_far(n)

    def wait_deep(n):
        columns = pl.ds(0, len(DEEP[n]) * WIDTH)
        wait_bytes(w_deep.at[pl.ds(0, WIDTH), columns], w_near.at[n])
        wait_bytes(w_deep.at[pl.ds(0, 3 * WIDTH), columns], w_far.at[n])

    def deep(h, n):
        first = slots[DEEP[n][0]] * WIDTH
        return jnp.dot(
            g_rows[h], w_deep[:, first : first + len(DEEP[n]) * WIDTH], preferred_element_type=F32
        )

    def flat(h, n):
        return jnp.dot(
            g_rows[h, :, : 2 * WIDTH], w_flat[:, n * 2 * WIDTH : (n + 1) * 2 * WIDTH],
            preferred_element_type=F32,
        )

    def give(kind, h, c, value, distance):
        piece = pl.ds(c * PIECE, PIECE)
        out_send[kind, h, piece, :] = value.astype(BF)
        target = chan(1 - yh, z, core) if kind >= OVER2 else chan(yh, z + distance, core)
        remote(
            out_send.at[kind, h, piece, :], out_recv.at[kind, h, piece, :],
            send_sem.at[5], out_sem.at[(2 * kind + h) * SUB + c], (s, target),
        )

    def take(kind, h, c):
        piece = pl.ds(c * PIECE, PIECE)
        wait_bytes(out_recv.at[kind, h, piece, :], out_sem.at[(2 * kind + h) * SUB + c])
        return out_recv[kind, h, piece, :].astype(F32)

    def cut(value, c):
        return value[c * PIECE : (c + 1) * PIECE]

    def relay(h):
        if h != RELAYED:
            return
        wait_bytes(g_recv.at[h, pl.ds(0, 2 * WIDTH - GROUP), :], g_sem.at[h])
        for yr in range(2):
            remote(
                g_recv.at[h, w_rows(yr), :], g_recv.at[h, w_rows(yr), :], send_sem.at[6],
                relay_sem, (s, mate),
            )

    def turn(h):
        if h == RELAYED:
            wait_bytes(g_recv.at[h, pl.ds(0, 2 * WIDTH), :], relay_sem)
        else:
            wait_bytes(g_recv.at[h, pl.ds(0, 4 * WIDTH - GROUP), :], g_sem.at[h])
        g_rows[h] = g_recv[h].astype(F32).T.astype(BF)

    def first(h):
        both = deep(h, 0)
        for c in range(SUB):
            give(R4, h, c, cut(both[:, :WIDTH], c), 2 if h == 0 else -2)
            give(UP3, h, c, cut(both[:, WIDTH:], c), 1)

    def first_down(h):
        one = deep(h, 1)
        for c in range(SUB):
            give(DOWN3, h, c, cut(one, c), -1)

    def over(h):
        both = flat(h, 1)
        for c in range(SUB):
            give(OVER6, h, c, cut(both[:, WIDTH:], c), 0)
        for c in range(SUB):
            give(OVER2, h, c, cut(both[:, :WIDTH], c), 0)

    relay(0)
    wait_deep(0)
    wait_deep(1)
    turn(0)
    first(0)
    first_down(0)
    relay(1)
    wait_bytes(w_flat.at[pl.ds(0, WIDTH), :], w_near.at[3])
    wait_bytes(w_flat.at[pl.ds(0, WIDTH), :], w_far.at[3])
    over(0)
    turn(1)
    first(1)
    first_down(1)
    over(1)
    for h in range(2):
        both = flat(h, 0)
        part[0, h] = both[:, :WIDTH]
        part[1, h] = both[:, WIDTH:]
    wait_deep(2)
    for h in range(2):
        both = deep(h, 2)
        for c in range(SUB):
            give(DOWN1, h, c, cut(both[:, :WIDTH], c), -1)
        for c in range(SUB):
            give(UP1, h, c, cut(both[:, WIDTH:], c), 1)
    for h in range(2):
        both = flat(h, 2)
        part[2, h] = both[:, :WIDTH]
        for c in range(SUB):
            give(OVER0, h, c, cut(both[:, WIDTH:], c), 0)

    def second(kind, h):
        for c in range(SUB):
            piece = pl.ds(c * PIECE, PIECE)
            if kind == UP2:
                total = part[0, h, piece, :] + take(UP3, h, c) + take(OVER2, h, c)
            else:
                total = part[1, h, piece, :] + take(DOWN3, h, c) + take(OVER6, h, c)
            if (kind == UP2) == (h == 0):
                total = total + take(R4, h, c)
            give(kind, h, c, total, 2 if kind == UP2 else -2)

    second(DOWN2, 0)
    second(UP2, 0)
    second(UP2, 1)
    second(DOWN2, 1)
    for h in range(2):
        for c in range(SUB):
            piece = pl.ds(c * PIECE, PIECE)
            part[2, h, piece, :] = (
                part[2, h, piece, :] + take(UP1, h, c) + take(DOWN1, h, c) + take(OVER0, h, c)
            )
    for h in range(2):
        for c in range(SUB):
            piece = pl.ds(c * PIECE, PIECE)
            total = part[2, h, piece, :] + take(UP2, h, c) + take(DOWN2, h, c)
            out_ref[pl.ds(h * HALF + c * PIECE, PIECE), :] = total.astype(BF)

    wait_bytes(taps_recv.at[pl.ds(0, SEQ - 1)], send_sem.at[0])
    wait_bytes(m_recv.at[pl.ds(0, GROUP * (SEQ - 1)), :], send_sem.at[1])
    wait_bytes(q_recv.at[pl.ds(0, GROUP * (SEQ - 1)), :], send_sem.at[2])
    wait_bytes(w_deep.at[pl.ds(0, 3 * WIDTH), :], send_sem.at[3])
    wait_bytes(w_flat.at[pl.ds(0, WIDTH), :], send_sem.at[3])
    wait_bytes(g_recv.at[0, pl.ds(0, 2 * WIDTH - GROUP), :], send_sem.at[4])
    wait_bytes(g_recv.at[0, pl.ds(0, 4 * WIDTH - GROUP), :], send_sem.at[4])
    wait_bytes(g_recv.at[0, pl.ds(0, 2 * WIDTH), :], send_sem.at[6])
    wait_bytes(out_send, send_sem.at[5])


def body(query_in, key_in, value_in, filter_taps, skip_gain, out_weight):
    dma = pltpu.SemaphoreType.DMA
    hbm = pl.BlockSpec(memory_space=pltpu.MemorySpace.HBM)
    skip_gain = skip_gain.reshape(1, WIDTH)
    operands = (query_in, key_in, value_in, filter_taps, skip_gain, out_weight)
    operands = [pltpu.with_memory_space_constraint(x, pltpu.MemorySpace.HBM) for x in operands]
    return pl.pallas_call(
        kernel,
        out_shape=jax.ShapeDtypeStruct((ROWS, WIDTH), BF),
        in_specs=[hbm] * 6,
        out_specs=pl.BlockSpec(memory_space=pltpu.VMEM),
        scratch_shapes=[
            pltpu.VMEM((ROWS, WIDTH), BF),
            pltpu.VMEM((ROWS, WIDTH), BF),
            pltpu.VMEM((ROWS, WIDTH), BF),
            pltpu.VMEM((1, WIDTH), F32),
            pltpu.VMEM((4 * WIDTH, 5 * WIDTH), BF),
            pltpu.VMEM((2 * WIDTH, 6 * WIDTH), BF),
            pltpu.VMEM((WIDTH, ROWS), BF),
            pltpu.VMEM((WIDTH, ROWS), BF),
            pltpu.VMEM((WIDTH, ROWS), BF),
            pltpu.VMEM((WIDTH, ROWS), BF),
            pltpu.VMEM((SEQ, ROWS), BF),
            pltpu.VMEM((SEQ, 1, ROWS), F32),
            pltpu.VMEM((SEQ, 1, ROWS), F32),
            pltpu.VMEM((SEQ, ROWS, ROWS), BF),
            pltpu.VMEM((WIDTH, ROWS), F32),
            pltpu.VMEM((2, WIDTH, HALF), BF),
            pltpu.VMEM((2, 4 * WIDTH, HALF), BF),
            pltpu.VMEM((2, HALF, 4 * WIDTH), BF),
            pltpu.VMEM((3, 2, HALF, WIDTH), F32),
            pltpu.VMEM((10, 2, HALF, WIDTH), BF),
            pltpu.VMEM((10, 2, HALF, WIDTH), BF),
            dma((5,)),
            dma((4,)),
            dma((4,)),
            dma((3,)),
            dma((2,)),
            dma,
            dma((20 * SUB,)),
            dma((7,)),
        ],
        compiler_params=pltpu.CompilerParams(collective_id=0, has_side_effects=True, vmem_limit_bytes=24 * 1024 * 1024),
    )(*operands)


def solution(mesh):
    placed = (
        P("seq", "chan"),
        P("seq", "chan"),
        P("seq", "chan"),
        P("chan", "seq"),
        P("chan"),
        P("chan", None),
    )
    return jax.shard_map(
        body, mesh=mesh, in_specs=placed, out_specs=P("seq", "chan"), check_vma=False
    )
```

```python
import functools

import jax
import jax.numpy as jnp
from jax import lax
from jax.experimental import pallas as pl
from jax.experimental.pallas import tpu as pltpu
from jax.sharding import PartitionSpec as P

MESH = pl.DeviceIdType.MESH
BF = jnp.bfloat16
F32 = jnp.float32
SEQ = 8
RING = 8
ROWS = 256
WIDTH = 128
GROUP = 16
HALF = 128
DEEP = ((4, 3), (5,), (7, 1))
SHALLOW = (2, 6, 0)
FIRST = 2
SUB = 1
RELAYED = 1
PIECE = HALF // SUB
DELTAS = ((1, 2), (0, 2), (1, 1), (1, 3), (1, 0), (0, 1), (0, 3))
R4, UP3, DOWN3, UP1, DOWN1, UP2, DOWN2, OVER2, OVER6, OVER0 = range(10)


def aligned(value, multiple):
    return pl.multiple_of(value, multiple)


def wait_bytes(ref, sem):
    pltpu.make_async_copy(ref, ref, sem).wait()


def kernel(
    q_hbm, k_hbm, v_hbm, taps_hbm, gain_hbm, w_hbm, out_ref,
    q_in, k_in, v_in, gain, w_deep, w_flat,
    m_send, q_send, m_recv, q_recv, taps_in, taps_send, taps_recv, tmat, conv, g_send, g_recv, g_rows,
    part, out_send, out_recv,
    load_sem, w_near, w_far, a2a_sem, g_sem, relay_sem, out_sem, send_sem,
):
    s = lax.axis_index("seq")
    k = lax.axis_index("chan")
    core = k % 2
    z = (k // 2) % RING
    yh = k // (2 * RING)

    def chan(y, level, c):
        return y * (2 * RING) + ((level + RING) % RING) * 2 + c

    mate = chan(yh, z, 1 - core)
    sharing = [(chan(y, z, c), yr) for yr, y in ((1, 1 - yh), (0, yh)) for c in (1 - core, core)]
    x, ylo = s % 4, s // 4
    near = ((ylo + 1) % 2) * 4 + x
    peers = [((ylo + dy) % 2) * 4 + (x + dx) % 4 for dy, dx in DELTAS]
    far_rows = [(near, chan(1 - yh, z, c), c) for c in (core, 1 - core)]

    loads = [
        pltpu.make_async_copy(k_hbm, k_in, load_sem.at[0]),
        pltpu.make_async_copy(v_hbm, v_in, load_sem.at[1]),
        pltpu.make_async_copy(q_hbm, q_in, load_sem.at[2]),
        pltpu.make_async_copy(gain_hbm, gain, load_sem.at[3]),
        pltpu.make_async_copy(taps_hbm, taps_in, load_sem.at[4]),
    ]
    for load in loads:
        load.start()

    barrier = pltpu.get_barrier_semaphore()
    same_core = [(chan(1 - yh, z, core), 1), (k, 0)]
    greeted = [(p, c) for p in peers for c, _ in sharing]
    greeted += [(s, c) for c, _ in sharing[:3]]
    greeted += [(s, chan(yh, z + i, core)) for i in (1, -1, 2, -2)]
    for target in greeted:
        pl.semaphore_signal(barrier, inc=1, device_id=target, device_id_type=MESH)

    def remote(src, dst, send, recv, target):
        pltpu.make_async_remote_copy(
            src_ref=src, dst_ref=dst, send_sem=send, recv_sem=recv,
            device_id=target, device_id_type=MESH,
        ).start()


    def w_block(y, distance, c):
        block = chan(y, z + distance, c)
        return w_hbm.at[:, pl.ds(aligned(block * WIDTH, WIDTH), WIDTH)]

    def w_rows(yr):
        return pl.ds(aligned(yr * 2 * WIDTH + core * WIDTH, WIDTH), WIDTH)

    slots = {r: n for n, r in enumerate(r for group in DEEP for r in group)}

    def deep_slot(r, yr):
        return w_deep.at[w_rows(yr), pl.ds(slots[r] * WIDTH, WIDTH)]

    def flat_slot(n):
        return w_flat.at[w_rows(0), pl.ds(n * WIDTH, WIDTH)]

    flat_blocks = [(yh, r) for r in SHALLOW[:2]] + [(1 - yh, r) for r in SHALLOW[:2]]
    flat_blocks += [(yh, SHALLOW[2]), (1 - yh, SHALLOW[2])]

    loads[0].wait()
    loads[1].wait()
    mixed = (k_in[...].astype(F32) * v_in[...].astype(F32)).astype(BF)
    m_send[...] = mixed.astype(F32).T.astype(BF)
    mine = pl.ds(aligned(s * GROUP, GROUP), GROUP)
    loads[3].wait()
    loads[4].wait()
    for n in range(SEQ):
        taps_send[n] = taps_in[n : n + 1, :].astype(F32)
    taps_recv[s] = taps_send[s]

    pl.semaphore_wait(barrier, len(greeted))

    for p in peers:
        remote(taps_send.at[p], taps_recv.at[s], send_sem.at[0], a2a_sem.at[0], (p, k))
    for p in peers:
        rows = pl.ds(aligned(p * GROUP, GROUP), GROUP)
        remote(m_send.at[rows, :], m_recv.at[mine, :], send_sem.at[1], a2a_sem.at[1], (p, k))
    loads[2].wait()
    q_send[...] = q_in[...].astype(F32).T.astype(BF)
    for p in peers:
        rows = pl.ds(aligned(p * GROUP, GROUP), GROUP)
        remote(q_send.at[rows, :], q_recv.at[mine, :], send_sem.at[2], a2a_sem.at[2], (p, k))

    def send_far(n):
        for r in DEEP[n]:
            for seq, target, c in far_rows:
                remote(w_block(1 - yh, r, c), deep_slot(r, 1), send_sem.at[3], w_far.at[n], (seq, target))

    for n in range(FIRST):
        send_far(n)
    for n, group in enumerate(DEEP):
        for r in group:
            remote(w_block(yh, r, 1 - core), deep_slot(r, 0), send_sem.at[3], w_far.at[n], (s, mate))
    for n, (y, r) in enumerate(flat_blocks):
        remote(w_block(y, r, 1 - core), flat_slot(n), send_sem.at[3], w_far.at[3], (s, mate))

    m_recv[mine, :] = m_send[mine, :]
    q_recv[mine, :] = q_send[mine, :]
    for n, group in enumerate(DEEP):
        for r in group:
            pltpu.make_async_copy(w_block(yh, r, core), deep_slot(r, 0), w_near.at[n]).start()
    for n, (y, r) in enumerate(flat_blocks):
        pltpu.make_async_copy(w_block(y, r, core), flat_slot(n), w_near.at[3]).start()

    wait_bytes(taps_recv.at[pl.ds(0, SEQ - 1)], a2a_sem.at[0])
    row = lax.broadcasted_iota(jnp.int32, (ROWS, ROWS), 0)
    col = lax.broadcasted_iota(jnp.int32, (ROWS, ROWS), 1)
    upper = col >= row
    before = jnp.zeros((ROWS, ROWS), F32)
    for d in range(SEQ):
        spread = jnp.broadcast_to(taps_recv[d], (ROWS, ROWS))
        rolled = pltpu.roll(spread, 0, 1, stride=1, stride_axis=0)
        tmat[d] = jnp.where(upper, rolled, before).astype(BF)
        before = rolled

    lane = lax.broadcasted_iota(jnp.int32, (WIDTH, WIDTH), 1)
    line = lax.broadcasted_iota(jnp.int32, (WIDTH, WIDTH), 0)
    picked = jnp.where(lane == s * GROUP + line % GROUP, jnp.broadcast_to(gain[...], (WIDTH, WIDTH)), 0.0)
    row_gain = jnp.sum(picked, axis=1, keepdims=True)

    wait_bytes(m_recv.at[pl.ds(0, GROUP * (SEQ - 1)), :], a2a_sem.at[1])
    conv[...] = jnp.dot(m_recv[...], tmat[0], preferred_element_type=F32)
    for d in range(1, SEQ):
        kept = WIDTH - GROUP * d
        conv[GROUP * d :, :] += jnp.dot(m_recv[:kept, :], tmat[d], preferred_element_type=F32)
    wait_bytes(q_recv.at[pl.ds(0, GROUP * (SEQ - 1)), :], a2a_sem.at[2])
    gated = q_recv[...].astype(F32) * (conv[...] + row_gain * m_recv[...].astype(F32))
    for h in range(2):
        g_send[h] = gated[:, h * HALF : (h + 1) * HALF].astype(BF)

    def land(yr):
        return pl.ds(aligned(yr * 2 * WIDTH + core * WIDTH + s * GROUP, GROUP), GROUP)

    for h in range(2):
        targets = same_core if h == RELAYED else sharing
        for p in (*peers[:5], None, *peers[5:]):
            rows = mine if p is None else pl.ds(aligned(p * GROUP, GROUP), GROUP)
            for c, yr in targets if p is not None else targets[:-1]:
                remote(
                    g_send.at[h, rows, :], g_recv.at[h, land(yr), :], send_sem.at[4], g_sem.at[h],
                    (s if p is None else p, c),
                )
        g_recv[h, land(0), :] = g_send[h, mine, :]
    for n in range(FIRST, len(DEEP)):
        send_far(n)

    def wait_deep(n):
        columns = pl.ds(0, len(DEEP[n]) * WIDTH)
        wait_bytes(w_deep.at[pl.ds(0, WIDTH), columns], w_near.at[n])
        wait_bytes(w_deep.at[pl.ds(0, 3 * WIDTH), columns], w_far.at[n])

    def deep(h, n):
        first = slots[DEEP[n][0]] * WIDTH
        return jnp.dot(
            g_rows[h], w_deep[:, first : first + len(DEEP[n]) * WIDTH], preferred_element_type=F32
        )

    def flat(h, n):
        return jnp.dot(
            g_rows[h, :, : 2 * WIDTH], w_flat[:, n * 2 * WIDTH : (n + 1) * 2 * WIDTH],
            preferred_element_type=F32,
        )

    def give(kind, h, c, value, distance):
        piece = pl.ds(c * PIECE, PIECE)
        out_send[kind, h, piece, :] = value.astype(BF)
        target = chan(1 - yh, z, core) if kind >= OVER2 else chan(yh, z + distance, core)
        remote(
            out_send.at[kind, h, piece, :], out_recv.at[kind, h, piece, :],
            send_sem.at[5], out_sem.at[(2 * kind + h) * SUB + c], (s, target),
        )

    def take(kind, h, c):
        piece = pl.ds(c * PIECE, PIECE)
        wait_bytes(out_recv.at[kind, h, piece, :], out_sem.at[(2 * kind + h) * SUB + c])
        return out_recv[kind, h, piece, :].astype(F32)

    def cut(value, c):
        return value[c * PIECE : (c + 1) * PIECE]

    def relay(h):
        if h != RELAYED:
            return
        wait_bytes(g_recv.at[h, pl.ds(0, 2 * WIDTH - GROUP), :], g_sem.at[h])
        for yr in range(2):
            remote(
                g_recv.at[h, w_rows(yr), :], g_recv.at[h, w_rows(yr), :], send_sem.at[6],
                relay_sem, (s, mate),
            )

    def turn(h):
        if h == RELAYED:
            wait_bytes(g_recv.at[h, pl.ds(0, 2 * WIDTH), :], relay_sem)
        else:
            wait_bytes(g_recv.at[h, pl.ds(0, 4 * WIDTH - GROUP), :], g_sem.at[h])
        g_rows[h] = g_recv[h].astype(F32).T.astype(BF)

    def first(h):
        both = deep(h, 0)
        for c in range(SUB):
            give(R4, h, c, cut(both[:, :WIDTH], c), 2 if h == 0 else -2)
            give(UP3, h, c, cut(both[:, WIDTH:], c), 1)

    def first_down(h):
        one = deep(h, 1)
        for c in range(SUB):
            give(DOWN3, h, c, cut(one, c), -1)

    def over(h):
        both = flat(h, 1)
        for c in range(SUB):
            give(OVER6, h, c, cut(both[:, WIDTH:], c), 0)
        for c in range(SUB):
            give(OVER2, h, c, cut(both[:, :WIDTH], c), 0)

    relay(0)
    wait_deep(0)
    wait_deep(1)
    turn(0)
    first(0)
    first_down(0)
    relay(1)
    wait_bytes(w_flat.at[pl.ds(0, WIDTH), :], w_near.at[3])
    wait_bytes(w_flat.at[pl.ds(0, WIDTH), :], w_far.at[3])
    over(0)
    turn(1)
    first(1)
    first_down(1)
    over(1)
    for h in range(2):
        both = flat(h, 0)
        part[0, h] = both[:, :WIDTH]
        part[1, h] = both[:, WIDTH:]
    wait_deep(2)
    for h in range(2):
        both = deep(h, 2)
        for c in range(SUB):
            give(DOWN1, h, c, cut(both[:, :WIDTH], c), -1)
        for c in range(SUB):
            give(UP1, h, c, cut(both[:, WIDTH:], c), 1)
    for h in range(2):
        both = flat(h, 2)
        part[2, h] = both[:, :WIDTH]
        for c in range(SUB):
            give(OVER0, h, c, cut(both[:, WIDTH:], c), 0)

    def second(kind, h):
        for c in range(SUB):
            piece = pl.ds(c * PIECE, PIECE)
            if kind == UP2:
                total = part[0, h, piece, :] + take(UP3, h, c) + take(OVER2, h, c)
            else:
                total = part[1, h, piece, :] + take(DOWN3, h, c) + take(OVER6, h, c)
            if (kind == UP2) == (h == 0):
                total = total + take(R4, h, c)
            give(kind, h, c, total, 2 if kind == UP2 else -2)

    second(DOWN2, 0)
    second(UP2, 0)
    second(UP2, 1)
    second(DOWN2, 1)
    for h in range(2):
        for c in range(SUB):
            piece = pl.ds(c * PIECE, PIECE)
            part[2, h, piece, :] = (
                part[2, h, piece, :] + take(UP1, h, c) + take(DOWN1, h, c) + take(OVER0, h, c)
            )
    for h in range(2):
        for c in range(SUB):
            piece = pl.ds(c * PIECE, PIECE)
            total = part[2, h, piece, :] + take(UP2, h, c) + take(DOWN2, h, c)
            out_ref[pl.ds(h * HALF + c * PIECE, PIECE), :] = total.astype(BF)

    wait_bytes(taps_recv.at[pl.ds(0, SEQ - 1)], send_sem.at[0])
    wait_bytes(m_recv.at[pl.ds(0, GROUP * (SEQ - 1)), :], send_sem.at[1])
    wait_bytes(q_recv.at[pl.ds(0, GROUP * (SEQ - 1)), :], send_sem.at[2])
    wait_bytes(w_deep.at[pl.ds(0, 3 * WIDTH), :], send_sem.at[3])
    wait_bytes(w_flat.at[pl.ds(0, WIDTH), :], send_sem.at[3])
    wait_bytes(g_recv.at[0, pl.ds(0, 2 * WIDTH - GROUP), :], send_sem.at[4])
    wait_bytes(g_recv.at[0, pl.ds(0, 4 * WIDTH - GROUP), :], send_sem.at[4])
    wait_bytes(g_recv.at[0, pl.ds(0, 2 * WIDTH), :], send_sem.at[6])
    wait_bytes(out_send, send_sem.at[5])


def body(query_in, key_in, value_in, filter_taps, skip_gain, out_weight):
    dma = pltpu.SemaphoreType.DMA
    hbm = pl.BlockSpec(memory_space=pltpu.MemorySpace.HBM)
    skip_gain = skip_gain.reshape(1, WIDTH)
    operands = (query_in, key_in, value_in, filter_taps, skip_gain, out_weight)
    operands = [pltpu.with_memory_space_constraint(x, pltpu.MemorySpace.HBM) for x in operands]
    return pl.pallas_call(
        kernel,
        out_shape=jax.ShapeDtypeStruct((ROWS, WIDTH), BF),
        in_specs=[hbm] * 6,
        out_specs=pl.BlockSpec(memory_space=pltpu.VMEM),
        scratch_shapes=[
            pltpu.VMEM((ROWS, WIDTH), BF),
            pltpu.VMEM((ROWS, WIDTH), BF),
            pltpu.VMEM((ROWS, WIDTH), BF),
            pltpu.VMEM((1, WIDTH), F32),
            pltpu.VMEM((4 * WIDTH, 5 * WIDTH), BF),
            pltpu.VMEM((2 * WIDTH, 6 * WIDTH), BF),
            pltpu.VMEM((WIDTH, ROWS), BF),
            pltpu.VMEM((WIDTH, ROWS), BF),
            pltpu.VMEM((WIDTH, ROWS), BF),
            pltpu.VMEM((WIDTH, ROWS), BF),
            pltpu.VMEM((SEQ, ROWS), BF),
            pltpu.VMEM((SEQ, 1, ROWS), F32),
            pltpu.VMEM((SEQ, 1, ROWS), F32),
            pltpu.VMEM((SEQ, ROWS, ROWS), BF),
            pltpu.VMEM((WIDTH, ROWS), F32),
            pltpu.VMEM((2, WIDTH, HALF), BF),
            pltpu.VMEM((2, 4 * WIDTH, HALF), BF),
            pltpu.VMEM((2, HALF, 4 * WIDTH), BF),
            pltpu.VMEM((3, 2, HALF, WIDTH), F32),
            pltpu.VMEM((10, 2, HALF, WIDTH), BF),
            pltpu.VMEM((10, 2, HALF, WIDTH), BF),
            dma((5,)),
            dma((4,)),
            dma((4,)),
            dma((3,)),
            dma((2,)),
            dma,
            dma((20 * SUB,)),
            dma((7,)),
        ],
        compiler_params=pltpu.CompilerParams(collective_id=0, has_side_effects=True, vmem_limit_bytes=24 * 1024 * 1024),
    )(*operands)


def solution(mesh):
    placed = (
        P("seq", "chan"),
        P("seq", "chan"),
        P("seq", "chan"),
        P("chan", "seq"),
        P("chan"),
        P("chan", None),
    )
    return jax.shard_map(
        body, mesh=mesh, in_specs=placed, out_specs=P("seq", "chan"), check_vma=False
    )
```
